32 devices in a mesh: groups: 2 (over y), mem: 8 (over z, x), lat: 2 (over core).
Axes of the slice: x: 2, y: 2, z: 4, core: 2. Of those that a mesh axis runs over, the one named last changes fastest.
Arguments:
- ensemble: float32 [16, 6, 256, 512], P(('groups', 'mem'), None, 'lat'), parts along dimension 0, may hold values from -1.5 to 1.5
- forcing_table: float32 [8, 256, 512], P(None, 'lat'), may hold values from -3 to 3
- ancestors: int32 [16], P('groups'), parts along dimension 0, may hold values from 0 to 7
- selector: int32 [16], P(('groups', 'mem')), parts along dimension 0, may hold values from 0 to 7
Outputs:
- advanced: float32 [16, 6, 256, 512], P(('groups', 'mem'), None, 'lat'), parts along dimension 0
The draws below stay inside these ranges and needn't reach their ends.
There are 2 independent parts, one for each index of `groups`. The reference program is written for one: setup_inputs(seed, part) draws one part's arguments, and reference() takes and returns one part's arrays. A program takes and returns all parts, laid end to end along the dimension named above; an argument that names none is the same for every part. Nothing has to cross between parts.
Inputs may be any that keep to these rules, and one draw needn't show every extreme that they name: `ancestors`: index of a member of the same ensemble; some parents are named by several slots, many by none. `selector`: index of a forcing pattern.
All inputs are finite; a program needn't handle non-finite values.
Results may differ from the reference program's by a relative error of at most 0.00002.
Values sent between devices are 32-bit elements; how exact they have to be, the bound alone decides.
No kernel may reach another device: no remote copies, remote signals or barrier semaphores. Data moves between devices by JAX's collectives and lax.ppermute only.
A program may use at most 192 MiB of HBM per device.

```python
import math
import jax
import jax.numpy as jnp
import numpy as np

MEMBERS = 8
NLAT = 256
NLON = 512
NFORCE = 8
STEPS = 3


def place_ends(drawn, rng, smallest, largest):
    longest = drawn.shape.index(max(drawn.shape))
    spots = []
    for shift in (0, 1):
        where = [jax.random.randint(jax.random.fold_in(rng, axis), (), 0, length) for axis, length in enumerate(drawn.shape)]
        where[longest] = (where[longest] + shift) % drawn.shape[longest]
        spots.append(tuple(where))
    return drawn.at[spots[0]].set(smallest).at[spots[1]].set(largest)


def block_scale(own_key, dims, split, low, largest):
    def one(axis_at, parts):
        draws = jax.random.uniform(jax.random.fold_in(jax.random.fold_in(own_key, 6), axis_at), (parts,), jnp.float32, low / len(split), largest / len(split))
        return jnp.repeat(jnp.exp(draws), dims[axis_at] // parts).reshape((-1,) + (1,) * (len(dims) - axis_at - 1))

    factor_of = one(*split[0])
    for cut in split[1:]:
        factor_of = factor_of * one(*cut)
    return factor_of


def rank_bounds(count, slope):
    weights = [(1 << 20) // math.isqrt(rank ** slope) + 1 for rank in range(1, count + 1)]
    width = 1 + sum(weights) // (1 << 30)
    return np.cumsum(np.array([max(1, weight // width) for weight in weights]))


def ranked_ids(rng, dims, count, skew):
    table = rank_bounds(count, skew)
    lot = jax.random.randint(jax.random.fold_in(rng, 1), dims, 0, int(table[count - 1]))
    rank = jnp.searchsorted(jnp.asarray(table, jnp.int32), lot, side="right")
    return jax.random.permutation(jax.random.fold_in(rng, 2), count)[rank].astype(jnp.int32)


def normal_values(own_key, shape, deviation, most, shards=(), kind=jnp.bfloat16):
    result = jax.random.normal(own_key, shape, jnp.float32) * deviation
    if len(shards) > 0:
        result = block_scale(own_key, shape, shards, -0.22, 0.18) * result
    return jnp.clip(result, min=-most, max=most).astype(kind)


def setup_inputs(seed: int = 0, part: int = 0) -> dict:
    arg_keys = jax.random.split(jax.random.key(seed), 5)
    part_splits = jax.random.split(jax.random.fold_in(arg_keys[4], part), 5)
    return {
        "ensemble": normal_values(part_splits[0], (MEMBERS, 6, NLAT, NLON), 0.3, 1.5, ((0, 8), (2, 2)), jnp.float32),
        "forcing_table": normal_values(arg_keys[1], (NFORCE, NLAT, NLON), 0.5, 3.0, ((1, 2),), jnp.float32),
        "ancestors": place_ends(ranked_ids(part_splits[2], (MEMBERS,), MEMBERS, 2), jax.random.fold_in(part_splits[2], 3), 0, MEMBERS - 1).astype(jnp.int32),
        "selector": place_ends(jax.random.randint(part_splits[3], (MEMBERS,), 0, NFORCE), jax.random.fold_in(part_splits[3], 1), 0, NFORCE - 1).astype(jnp.int32),
    }


TIME_STEP = 0.25
DENSITY_RATIO = 0.9
DRAG_RATE = 0.1
CORIOLIS_MEAN = 0.5


def row_below(values):
    widths = [(0, 0)] * (values.ndim - 2) + [(1, 0), (0, 0)]
    return jnp.pad(values[..., :-1, :], widths)


def row_above(values):
    widths = [(0, 0)] * (values.ndim - 2) + [(0, 1), (0, 0)]
    return jnp.pad(values[..., 1:, :], widths)


def col_west(values):
    return jnp.roll(values, 1, axis=-1)


def col_east(values):
    return jnp.roll(values, -1, axis=-1)


def advance(fields, forcing, row_ids, total):
    inside = ((row_ids >= 0.0) & (row_ids < total)).astype(jnp.float32)[:, None]
    wall_mask = ((row_ids >= 1.0) & (row_ids < total)).astype(jnp.float32)[:, None]
    coriolis_u = CORIOLIS_MEAN + (row_ids / total - 0.5)[:, None]
    coriolis_v = CORIOLIS_MEAN + ((row_ids - 0.5) / total - 0.5)[:, None]
    heights = []
    zonal = []
    merid = []
    for layer_index in range(2):
        height = fields[:, 3 * layer_index]
        speed_u = fields[:, 3 * layer_index + 1]
        speed_v = fields[:, 3 * layer_index + 2] * wall_mask
        thickness = 1.0 + height
        flux_x = speed_u * (0.5 * (thickness + col_west(thickness)))
        flux_y = speed_v * (0.5 * (thickness + row_below(thickness)))
        divergence = (col_east(flux_x) - flux_x) + (row_above(flux_y) - flux_y)
        heights.append(height - TIME_STEP * divergence)
        zonal.append(speed_u)
        merid.append(speed_v)
    pressures = [heights[0] + heights[1], DENSITY_RATIO * heights[0] + heights[1]]
    outputs = []
    for layer_index in range(2):
        speed_u = zonal[layer_index]
        speed_v = merid[layer_index]
        pressure = pressures[layer_index]
        extra = forcing if layer_index == 0 else -DRAG_RATE * speed_u
        above_v = row_above(speed_v)
        mean_v = 0.25 * (speed_v + col_west(speed_v) + above_v + col_west(above_v))
        new_u = speed_u + TIME_STEP * (coriolis_u * mean_v - (pressure - col_west(pressure)) + extra)
        below_u = row_below(speed_u)
        mean_u = 0.25 * (speed_u + col_east(speed_u) + below_u + col_east(below_u))
        new_v = (speed_v + TIME_STEP * (-coriolis_v * mean_u - (pressure - row_below(pressure)))) * wall_mask
        outputs.extend([heights[layer_index] * inside, new_u * inside, new_v * inside])
    return jnp.stack(outputs, axis=1)


def reference(ensemble, forcing_table, ancestors, selector):
    parents = jnp.take(ensemble, ancestors, axis=0)
    patterns = jnp.arange(NFORCE, dtype=jnp.int32)
    chosen = selector[:, None, None, None] == patterns[None, :, None, None]
    slot_forcing = jnp.sum(jnp.where(chosen, forcing_table[None], jnp.float32(0.0)), axis=1)
    row_ids = jnp.arange(NLAT).astype(jnp.float32)
    total = jnp.float32(NLAT)
    fields = parents
    for step_index in range(STEPS):
        fields = advance(fields, slot_forcing, row_ids, total)
    return fields
```

```python
import functools

import jax
import jax.numpy as jnp
from jax import lax
from jax.experimental import pallas as pl
from jax.experimental.pallas import tpu as pltpu
from jax.sharding import PartitionSpec as P

STEPS = 3


TIME_STEP = 0.25
DENSITY_RATIO = 0.9
DRAG_RATE = 0.1
CORIOLIS_MEAN = 0.5

TILE = 8


def copy_members(block, ancestors):
    slots, fields_count, band_rows, columns = block.shape
    count = lax.axis_size("mem")
    pieces = block.reshape(count, slots * fields_count * band_rows // count, columns)
    spread = lax.all_to_all(pieces, "mem", split_axis=0, concat_axis=0, tiled=True)
    taken = jnp.take(spread, ancestors, axis=0, mode="clip")
    moved = lax.all_to_all(taken, "mem", split_axis=0, concat_axis=0, tiled=True)
    return moved.reshape(slots * fields_count, band_rows, columns)


def edge_rows(block):
    rows = block.shape[-2]
    dim = block.ndim - 2
    count = lax.axis_size("lat")
    place = lax.axis_index("lat")
    if count == 2:
        sent = lax.dynamic_slice_in_dim(block, (1 - place) * (rows - TILE), TILE, axis=dim)
        got = lax.ppermute(sent, "lat", [(0, 1), (1, 0)])
        return jnp.where(place > 0, got, 0.0), jnp.where(place < 1, got, 0.0)
    forward = [(i, i + 1) for i in range(count - 1)]
    backward = [(target, source) for source, target in forward]
    below = lax.ppermute(lax.slice_in_dim(block, rows - TILE, rows, axis=dim), "lat", forward)
    above = lax.ppermute(lax.slice_in_dim(block, 0, TILE, axis=dim), "lat", backward)
    return below, above


def stencil_kernel(count, place_ref, parent_ref, low_ref, high_ref, force_ref, force_low_ref, force_high_ref, out_ref, first, second, force):
    rows, columns = parent_ref.shape[1:]
    blocks = rows // TILE
    place = place_ref[0]
    total = float(rows * count)
    tile = (TILE, columns)
    sub = lax.broadcasted_iota(jnp.int32, tile, 0)
    top = sub == TILE - 1
    bottom = sub == 0

    for field in range(6):
        low, mid, high = low_ref[field], parent_ref[field], high_ref[field]
        if field % 3 == 2:
            wall = lax.broadcasted_iota(jnp.int32, mid.shape, 0) + place * rows > 0
            mid = jnp.where(wall, mid, 0.0)
        first[field, :TILE] = low
        first[field, TILE : TILE + rows] = mid
        first[field, TILE + rows :] = high
        second[field, :TILE] = low
        second[field, TILE + rows :] = high
    force[:TILE] = force_low_ref[...]
    force[TILE : TILE + rows] = force_ref[...]
    force[TILE + rows :] = force_high_ref[...]

    def at(block):
        return pl.ds(pl.multiple_of(block * TILE, TILE), TILE)

    def down(here, before):
        return jnp.where(bottom, pltpu.roll(before, 1, 0), pltpu.roll(here, 1, 0))

    def up(here, after):
        return jnp.where(top, pltpu.roll(after, TILE - 1, 0), pltpu.roll(here, TILE - 1, 0))

    def west(values):
        return pltpu.roll(values, 1, 1)

    def east(values):
        return pltpu.roll(values, columns - 1, 1)

    def heights(source, block):
        prev, here, after = at(jnp.maximum(block - 1, 0)), at(block), at(jnp.minimum(block + 1, blocks + 1))
        result = []
        for base in (0, 3):
            height = source[base, here]
            speed_u = source[base + 1, here]
            speed_v = source[base + 2, here]
            above_v = up(speed_v, source[base + 2, after])
            thick = 1.0 + height
            below_thick = 1.0 + down(height, source[base, prev])
            above_thick = 1.0 + up(height, source[base, after])
            flux_x = speed_u * (0.5 * (thick + west(thick)))
            flux_y = speed_v * (0.5 * (thick + below_thick))
            above_flux = above_v * (0.5 * (above_thick + thick))
            divergence = (east(flux_x) - flux_x) + (above_flux - flux_y)
            result.append((height - TIME_STEP * divergence, speed_u, speed_v, above_v))
        return result

    def block_step(source, target, shift, block, before):
        prev, here = at(jnp.maximum(block - 1, 0)), at(block)
        there = at(block - shift)
        parts = heights(source, block)
        row = (sub + ((block - 1) * TILE + place * rows)).astype(jnp.float32)
        coriolis_u = CORIOLIS_MEAN + (row * (1.0 / total) - 0.5)
        coriolis_v = CORIOLIS_MEAN + ((row - 0.5) * (1.0 / total) - 0.5)
        wall = row >= 1.0
        new = [part[0] for part in parts]
        ratios = (1.0, DENSITY_RATIO)
        for layer in range(2):
            base = 3 * layer
            _, speed_u, speed_v, above_v = parts[layer]
            if layer == 0:
                pressure = new[0] + new[1]
                below_pressure = before[0] + before[1]
                extra = force[here]
            else:
                pressure = DENSITY_RATIO * new[0] + new[1]
                below_pressure = DENSITY_RATIO * before[0] + before[1]
                extra = -DRAG_RATE * speed_u
            sum_v = speed_v + above_v
            mean_v = 0.25 * (sum_v + west(sum_v))
            new_u = speed_u + TIME_STEP * (coriolis_u * mean_v - (pressure - west(pressure)) + extra)
            sum_u = speed_u + down(speed_u, source[base + 1, prev])
            mean_u = 0.25 * (sum_u + east(sum_u))
            slope = pressure - down(pressure, below_pressure)
            new_v = speed_v + TIME_STEP * (-coriolis_v * mean_u - slope)
            target[base, there] = new[layer]
            target[base + 1, there] = new_u
            target[base + 2, there] = jnp.where(wall, new_v, 0.0)
        return tuple(new)

    start = jnp.where(place == 0, 1, 0)
    stop = jnp.where(place == count - 1, blocks + 1, blocks + 2)
    zero = jnp.zeros(tile, jnp.float32)
    source, target = first, second
    for _ in range(STEPS - 1):
        lax.fori_loop(start, stop, functools.partial(block_step, source, target, 0), (zero, zero))
        source, target = target, source
    edge = heights(source, 0)
    lax.fori_loop(1, blocks + 1, functools.partial(block_step, source, out_ref, 1), (edge[0][0], edge[1][0]))


def stencil(place, parents, low, high, forcing, force_low, force_high):
    fields_count, rows, columns = parents.shape
    grown = rows + 2 * TILE
    vmem = pl.BlockSpec(memory_space=pltpu.VMEM)
    return pl.pallas_call(
        functools.partial(stencil_kernel, lax.axis_size("lat")),
        out_shape=jax.ShapeDtypeStruct(parents.shape, jnp.float32),
        in_specs=[pl.BlockSpec(memory_space=pltpu.SMEM)] + [vmem] * 6,
        out_specs=vmem,
        scratch_shapes=[
            pltpu.VMEM((fields_count, grown, columns), jnp.float32),
            pltpu.VMEM((fields_count, grown, columns), jnp.float32),
            pltpu.VMEM((grown, columns), jnp.float32),
        ],
        cost_estimate=pl.CostEstimate(flops=300 * rows * columns, bytes_accessed=52 * rows * columns, transcendentals=0),
    )(place, parents, low, high, forcing, force_low, force_high)


def on_device(ensemble, forcing_table, ancestors, selector):
    forcing = lax.dynamic_index_in_dim(forcing_table, selector[0], 0, keepdims=False)
    force_low, force_high = edge_rows(forcing)
    parents = copy_members(ensemble, ancestors)
    low, high = edge_rows(parents)
    place = lax.axis_index("lat").astype(jnp.int32)[None]
    result = stencil(place, parents, low, high, forcing, force_low, force_high)
    return result.reshape(ensemble.shape)


def solution(mesh):
    placed = (
        P(("groups", "mem"), None, "lat", None),
        P(None, "lat", None),
        P("groups"),
        P(("groups", "mem")),
    )
    return jax.shard_map(
        on_device,
        mesh=mesh,
        in_specs=placed,
        out_specs=P(("groups", "mem"), None, "lat", None),
        check_vma=False,
    )
```

```python
import functools

import jax
import jax.numpy as jnp
from jax import lax
from jax.experimental import pallas as pl
from jax.experimental.pallas import tpu as pltpu
from jax.sharding import PartitionSpec as P

STEPS = 3


TIME_STEP = 0.25
DENSITY_RATIO = 0.9
DRAG_RATE = 0.1
CORIOLIS_MEAN = 0.5

TILE = 8
LANES = 128


def copy_members(block, ancestors):
    slots, fields_count, band_rows, columns = block.shape
    count = lax.axis_size("mem")
    pieces = block.reshape(count, slots * fields_count * band_rows // count, columns)
    spread = lax.all_to_all(pieces, "mem", split_axis=0, concat_axis=0, tiled=True)
    taken = jnp.take(spread, ancestors, axis=0, mode="clip")
    moved = lax.all_to_all(taken, "mem", split_axis=0, concat_axis=0, tiled=True)
    return moved.reshape(slots * fields_count, band_rows, columns)


def edge_rows(block):
    rows = block.shape[-2]
    dim = block.ndim - 2
    count = lax.axis_size("lat")
    place = lax.axis_index("lat")
    if count == 2:
        sent = lax.dynamic_slice_in_dim(block, (1 - place) * (rows - TILE), TILE, axis=dim)
        got = lax.ppermute(sent, "lat", [(0, 1), (1, 0)])
        return jnp.where(place > 0, got, 0.0), jnp.where(place < 1, got, 0.0)
    forward = [(i, i + 1) for i in range(count - 1)]
    backward = [(target, source) for source, target in forward]
    below = lax.ppermute(lax.slice_in_dim(block, rows - TILE, rows, axis=dim), "lat", forward)
    above = lax.ppermute(lax.slice_in_dim(block, 0, TILE, axis=dim), "lat", backward)
    return below, above


def stencil_kernel(count, place_ref, parent_ref, low_ref, high_ref, force_ref, force_low_ref, force_high_ref, out_ref, first, second, force):
    rows, columns = parent_ref.shape[1:]
    blocks = rows // TILE
    strips = columns // LANES
    place = place_ref[0]
    total = float(rows * count)
    tile = (TILE, LANES)
    sub = lax.broadcasted_iota(jnp.int32, tile, 0)
    lane = lax.broadcasted_iota(jnp.int32, tile, 1)
    bottom = sub == 0
    left = lane == 0
    right = lane == LANES - 1
    zero = jnp.zeros(tile, jnp.float32)
    head = 2 * TILE
    last = head + rows

    for strip in range(strips):
        span = slice(strip * LANES, (strip + 1) * LANES)
        for field in range(6):
            for buffer in (first, second):
                buffer[field, strip, :TILE] = zero
                buffer[field, strip, last + TILE :] = zero
                buffer[field, strip, TILE:head] = low_ref[field, :, span]
                buffer[field, strip, last : last + TILE] = high_ref[field, :, span]
            first[field, strip, head:last] = parent_ref[field, :, span]
            if field % 3 == 2:
                edge = first[field, strip, head : head + TILE]
                first[field, strip, head : head + TILE] = jnp.where(sub + place > 0, edge, 0.0)
        force[strip, TILE:head] = TIME_STEP * force_low_ref[:, span]
        force[strip, head:last] = TIME_STEP * force_ref[:, span]
        force[strip, last : last + TILE] = TIME_STEP * force_high_ref[:, span]

    def west(values):
        turned = [pltpu.roll(value, 1, 1) for value in values]
        return [jnp.where(left, turned[i - 1], turned[i]) for i in range(strips)]

    def east(values):
        turned = [pltpu.roll(value, LANES - 1, 1) for value in values]
        return [jnp.where(right, turned[(i + 1) % strips], turned[i]) for i in range(strips)]

    def load(source, field, block, offset=0):
        return [source[field, strip, pl.ds(TILE * (block + 1) + offset, TILE)] for strip in range(strips)]

    def each(function, *lists):
        return [function(*items) for items in zip(*lists)]

    def weight(values):
        return [0.5 * TIME_STEP + (0.5 * TIME_STEP) * value for value in values]

    def heights(source, block):
        result = []
        for base in (0, 3):
            height = load(source, base, block)
            speed_u = load(source, base + 1, block)
            speed_v = load(source, base + 2, block)
            above_v = load(source, base + 2, block, 1)
            thick = weight(height)
            below = weight(load(source, base, block, -1))
            above = weight(load(source, base, block, 1))
            flux_x = each(lambda u, t, w: u * (t + w), speed_u, thick, west(thick))
            flux_y = each(lambda v, t, b: v * (t + b), speed_v, thick, below)
            above_flux = each(lambda v, t, a: v * (a + t), above_v, thick, above)
            new = each(lambda h, e, x, a, y: h - ((e - x) + (a - y)), height, east(flux_x), flux_x, above_flux, flux_y)
            result.append((new, speed_u, speed_v, above_v))
        return result

    def scaled_pressures(parts):
        upper = [TIME_STEP * value for value in parts[0][0]]
        lower = [TIME_STEP * value for value in parts[1][0]]
        return each(lambda a, b: a + b, upper, lower), each(lambda a, b: DENSITY_RATIO * a + b, upper, lower)

    def turn(values):
        return [pltpu.roll(value, 1, 0) for value in values]

    def block_step(source, store, block, carried):
        parts = heights(source, block)
        pressures = scaled_pressures(parts)
        row = (sub + ((block - 1) * TILE + place * rows)).astype(jnp.float32)
        coriolis_u = (0.25 * TIME_STEP) * (CORIOLIS_MEAN + (row * (1.0 / total) - 0.5))
        coriolis_v = (0.25 * TIME_STEP) * (CORIOLIS_MEAN + ((row - 0.5) * (1.0 / total) - 0.5))
        keep = []
        for layer in range(2):
            base = 3 * layer
            height, speed_u, speed_v, above_v = parts[layer]
            pressure = pressures[layer]
            sum_v = each(lambda v, a: v + a, speed_v, above_v)
            if layer == 0:
                forced = [speed_u[strip] + force[strip, pl.ds(pl.multiple_of(TILE * (block + 1), TILE), TILE)] for strip in range(strips)]
            else:
                forced = [(1.0 - TIME_STEP * DRAG_RATE) * value for value in speed_u]
            new_u = each(lambda f, s, ws, p, wp: (f + coriolis_u * (s + ws)) - (p - wp), forced, sum_v, west(sum_v), pressure, west(pressure))
            sum_u = each(lambda u, b: u + b, speed_u, load(source, base + 1, block, -1))
            turned = turn(pressure)
            below_pressure = each(lambda b, t: jnp.where(bottom, b, t), carried[layer], turned)
            keep.append(turned)
            new_v = each(lambda v, s, es, p, bp: (v - coriolis_v * (s + es)) - (p - bp), speed_v, sum_u, east(sum_u), pressure, below_pressure)
            store(base, block, height)
            store(base + 1, block, new_u)
            store(base + 2, block, new_v)
        return keep

    def into(target):
        def store(field, block, values):
            for strip in range(strips):
                target[field, strip, pl.ds(pl.multiple_of(TILE * (block + 1), TILE), TILE)] = values[strip]

        return store

    def out(field, block, values):
        for strip in range(strips):
            out_ref[field, pl.ds(pl.multiple_of(TILE * (block - 1), TILE), TILE), strip * LANES : (strip + 1) * LANES] = values[strip]

    start = jnp.where(place == 0, 1, 0)
    stop = jnp.where(place == count - 1, blocks + 1, blocks + 2)
    source, target = first, second
    for _ in range(STEPS - 1):
        lax.fori_loop(start, stop, functools.partial(block_step, source, into(target)), [[zero] * strips] * 2)

        @pl.when(place == 0)
        def _():
            for field in (2, 5):
                for strip in range(strips):
                    target[field, strip, head : head + TILE] = jnp.where(bottom, 0.0, target[field, strip, head : head + TILE])

        source, target = target, source
    edge = [turn(values) for values in scaled_pressures(heights(source, 0))]
    lax.fori_loop(1, blocks + 1, functools.partial(block_step, source, out), edge)

    @pl.when(place == 0)
    def _():
        for field in (2, 5):
            for strip in range(strips):
                span = slice(strip * LANES, (strip + 1) * LANES)
                out_ref[field, :TILE, span] = jnp.where(bottom, 0.0, out_ref[field, :TILE, span])


def stencil(place, parents, low, high, forcing, force_low, force_high):
    fields_count, rows, columns = parents.shape
    shape = (fields_count, columns // LANES, rows + 4 * TILE, LANES)
    vmem = pl.BlockSpec(memory_space=pltpu.VMEM)
    return pl.pallas_call(
        functools.partial(stencil_kernel, lax.axis_size("lat")),
        out_shape=jax.ShapeDtypeStruct(parents.shape, jnp.float32),
        in_specs=[pl.BlockSpec(memory_space=pltpu.SMEM)] + [vmem] * 6,
        out_specs=vmem,
        scratch_shapes=[pltpu.VMEM(shape, jnp.float32), pltpu.VMEM(shape, jnp.float32), pltpu.VMEM(shape[1:], jnp.float32)],
        compiler_params=pltpu.CompilerParams(vmem_limit_bytes=12 << 20),
        cost_estimate=pl.CostEstimate(flops=300 * rows * columns, bytes_accessed=52 * rows * columns, transcendentals=0),
    )(place, parents, low, high, forcing, force_low, force_high)


def on_device(ensemble, forcing_table, ancestors, selector):
    forcing = lax.dynamic_index_in_dim(forcing_table, selector[0], 0, keepdims=False)
    force_low, force_high = edge_rows(forcing)
    parents = copy_members(ensemble, ancestors)
    low, high = edge_rows(parents)
    place = lax.axis_index("lat").astype(jnp.int32)[None]
    result = stencil(place, parents, low, high, forcing, force_low, force_high)
    return result.reshape(ensemble.shape)


def solution(mesh):
    placed = (
        P(("groups", "mem"), None, "lat", None),
        P(None, "lat", None),
        P("groups"),
        P(("groups", "mem")),
    )
    return jax.shard_map(
        on_device,
        mesh=mesh,
        in_specs=placed,
        out_specs=P(("groups", "mem"), None, "lat", None),
        check_vma=False,
    )
```

```python
import functools

import jax
import jax.numpy as jnp
from jax import lax
from jax.experimental import pallas as pl
from jax.experimental.pallas import tpu as pltpu
from jax.sharding import PartitionSpec as P

STEPS = 3


TIME_STEP = 0.25
DENSITY_RATIO = 0.9
DRAG_RATE = 0.1
CORIOLIS_MEAN = 0.5

TILE = 8
LANES = 128


def copy_members(block, ancestors):
    slots, fields_count, band_rows, columns = block.shape
    count = lax.axis_size("mem")
    pieces = block.reshape(count, slots * fields_count * band_rows // count, columns)
    spread = lax.all_to_all(pieces, "mem", split_axis=0, concat_axis=0, tiled=True)
    taken = jnp.take(spread, ancestors, axis=0, mode="clip")
    moved = lax.all_to_all(taken, "mem", split_axis=0, concat_axis=0, tiled=True)
    return moved.reshape(slots * fields_count, band_rows, columns)


def edge_rows(block):
    rows = block.shape[-2]
    dim = block.ndim - 2
    count = lax.axis_size("lat")
    place = lax.axis_index("lat")
    if count == 2:
        sent = lax.dynamic_slice_in_dim(block, (1 - place) * (rows - TILE), TILE, axis=dim)
        got = lax.ppermute(sent, "lat", [(0, 1), (1, 0)])
        return jnp.where(place > 0, got, 0.0), jnp.where(place < 1, got, 0.0)
    forward = [(i, i + 1) for i in range(count - 1)]
    backward = [(target, source) for source, target in forward]
    below = lax.ppermute(lax.slice_in_dim(block, rows - TILE, rows, axis=dim), "lat", forward)
    above = lax.ppermute(lax.slice_in_dim(block, 0, TILE, axis=dim), "lat", backward)
    return below, above


HEIGHT_SCALE = TIME_STEP * TIME_STEP / 2
SPEED_SCALE = TIME_STEP / 2


def stencil_kernel(count, place_ref, parent_ref, low_ref, high_ref, force_ref, force_low_ref, force_high_ref, out_ref, first, second, force):
    rows, columns = parent_ref.shape[1:]
    blocks = rows // TILE
    strips = columns // LANES
    place = place_ref[0]
    total = float(rows * count)
    tile = (TILE, LANES)
    sub = lax.broadcasted_iota(jnp.int32, tile, 0)
    lane = lax.broadcasted_iota(jnp.int32, tile, 1)
    bottom = sub == 0
    left = lane == 0
    right = lane == LANES - 1
    zero = jnp.zeros(tile, jnp.float32)
    head = 2 * TILE
    last = head + rows

    def scaled(field, value):
        return HEIGHT_SCALE + HEIGHT_SCALE * value if field % 3 == 0 else SPEED_SCALE * value

    for strip in range(strips):
        span = slice(strip * LANES, (strip + 1) * LANES)
        for field in range(6):
            low = scaled(field, low_ref[field, :, span])
            high = scaled(field, high_ref[field, :, span])
            for buffer in (first, second):
                buffer[field, strip, :TILE] = zero
                buffer[field, strip, last + TILE : last + 2 * TILE] = zero
                buffer[field, strip, last + 2 * TILE :] = zero
                buffer[field, strip, TILE:head] = low
                buffer[field, strip, last : last + TILE] = high
            first[field, strip, head:last] = scaled(field, parent_ref[field, :, span])
            if field % 3 == 2:
                edge = first[field, strip, head : head + TILE]
                first[field, strip, head : head + TILE] = jnp.where(sub + place > 0, edge, 0.0)
        force[strip, TILE:head] = (TIME_STEP * SPEED_SCALE) * force_low_ref[:, span]
        force[strip, head:last] = (TIME_STEP * SPEED_SCALE) * force_ref[:, span]
        force[strip, last : last + TILE] = (TIME_STEP * SPEED_SCALE) * force_high_ref[:, span]

    def west(values):
        turned = [pltpu.roll(value, 1, 1) for value in values]
        return [jnp.where(left, turned[i - 1], turned[i]) for i in range(strips)]

    def east(values):
        turned = [pltpu.roll(value, LANES - 1, 1) for value in values]
        return [jnp.where(right, turned[(i + 1) % strips], turned[i]) for i in range(strips)]

    def load(source, field, block, offset=0):
        return [source[field, strip, pl.ds(TILE * (block + 1) + offset, TILE)] for strip in range(strips)]

    def each(function, *lists):
        return [function(*items) for items in zip(*lists)]

    def keep(target, field, block, values):
        for strip in range(strips):
            target[field, strip, pl.ds(pl.multiple_of(TILE * (block + 1), TILE), TILE)] = values[strip]

    def give(field, block, values):
        for strip in range(strips):
            value = values[strip] * (1.0 / HEIGHT_SCALE) - 1.0 if field % 3 == 0 else values[strip] * (1.0 / SPEED_SCALE)
            out_ref[field, pl.ds(pl.multiple_of(TILE * (block - 1), TILE), TILE), strip * LANES : (strip + 1) * LANES] = value

    def heights(source, target, block):
        for base in (0, 3):
            thick = load(source, base, block)
            flux_x = each(lambda u, t, w: u * (t + w), load(source, base + 1, block), thick, west(thick))
            flux_y = each(lambda v, t, b: v * (t + b), load(source, base + 2, block), thick, load(source, base, block, -1))
            above_flux = each(lambda v, t, a: v * (t + a), load(source, base + 2, block, 1), thick, load(source, base, block, 1))
            new = each(lambda h, e, x, a, y: (h - (e - x)) - (a - y), thick, east(flux_x), flux_x, above_flux, flux_y)
            keep(target, base, block, new)

    def speeds(source, target, block, store):
        row = (sub + ((block - 1) * TILE + place * rows)).astype(jnp.float32)
        coriolis_u = (0.25 * TIME_STEP) * (CORIOLIS_MEAN + (row * (1.0 / total) - 0.5))
        coriolis_v = (0.25 * TIME_STEP) * (CORIOLIS_MEAN + ((row - 0.5) * (1.0 / total) - 0.5))
        upper, lower = load(target, 0, block), load(target, 3, block)
        below_upper, below_lower = load(target, 0, block, -1), load(target, 3, block, -1)
        for layer in range(2):
            base = 3 * layer
            if layer == 0:
                pressure = each(lambda a, b: a + b, upper, lower)
                below_pressure = each(lambda a, b: a + b, below_upper, below_lower)
            else:
                pressure = each(lambda a, b: DENSITY_RATIO * a + b, upper, lower)
                below_pressure = each(lambda a, b: DENSITY_RATIO * a + b, below_upper, below_lower)
            speed_u = load(source, base + 1, block)
            speed_v = load(source, base + 2, block)
            turn_v = each(lambda v, a: coriolis_u * (v + a), speed_v, load(source, base + 2, block, 1))
            if layer == 0:
                forced = [speed_u[strip] + force[strip, pl.ds(pl.multiple_of(TILE * (block + 1), TILE), TILE)] for strip in range(strips)]
            else:
                forced = [(1.0 - TIME_STEP * DRAG_RATE) * value for value in speed_u]
            pushed = west(each(lambda t, p: t + p, turn_v, pressure))
            store(base + 1, block, each(lambda f, t, p, w: (f + (t - p)) + w, forced, turn_v, pressure, pushed))
            sum_u = each(lambda u, b: u + b, speed_u, load(source, base + 1, block, -1))
            slope = each(lambda p, b: p - b, pressure, below_pressure)
            store(base + 2, block, each(lambda v, s, es, d: (v - coriolis_v * (s + es)) - d, speed_v, sum_u, east(sum_u), slope))

    start = jnp.where(place == 0, 1, 0)
    stop = jnp.where(place == count - 1, blocks + 1, blocks + 2)
    source, target = first, second
    for _ in range(STEPS - 1):
        heights(source, target, start)

        def step(block, carry, source=source, target=target):
            heights(source, target, block + 1)
            speeds(source, target, block, functools.partial(keep, target))
            return carry

        lax.fori_loop(start, stop, step, 0)

        @pl.when(place == 0)
        def _():
            for field in (2, 5):
                for strip in range(strips):
                    target[field, strip, head : head + TILE] = jnp.where(bottom, 0.0, target[field, strip, head : head + TILE])

        source, target = target, source
    heights(source, target, 0)
    heights(source, target, 1)

    def finish(block, carry):
        heights(source, target, block + 1)
        give(0, block, load(target, 0, block))
        give(3, block, load(target, 3, block))
        speeds(source, target, block, give)
        return carry

    lax.fori_loop(1, blocks + 1, finish, 0)

    @pl.when(place == 0)
    def _():
        for field in (2, 5):
            for strip in range(strips):
                span = slice(strip * LANES, (strip + 1) * LANES)
                out_ref[field, :TILE, span] = jnp.where(bottom, 0.0, out_ref[field, :TILE, span])


def stencil(place, parents, low, high, forcing, force_low, force_high):
    fields_count, rows, columns = parents.shape
    shape = (fields_count, columns // LANES, rows + 5 * TILE, LANES)
    vmem = pl.BlockSpec(memory_space=pltpu.VMEM)
    return pl.pallas_call(
        functools.partial(stencil_kernel, lax.axis_size("lat")),
        out_shape=jax.ShapeDtypeStruct(parents.shape, jnp.float32),
        in_specs=[pl.BlockSpec(memory_space=pltpu.SMEM)] + [vmem] * 6,
        out_specs=vmem,
        scratch_shapes=[pltpu.VMEM(shape, jnp.float32), pltpu.VMEM(shape, jnp.float32), pltpu.VMEM(shape[1:], jnp.float32)],
        compiler_params=pltpu.CompilerParams(vmem_limit_bytes=12 << 20),
        cost_estimate=pl.CostEstimate(flops=300 * rows * columns, bytes_accessed=52 * rows * columns, transcendentals=0),
    )(place, parents, low, high, forcing, force_low, force_high)


def on_device(ensemble, forcing_table, ancestors, selector):
    forcing = lax.dynamic_index_in_dim(forcing_table, selector[0], 0, keepdims=False)
    force_low, force_high = edge_rows(forcing)
    parents = copy_members(ensemble, ancestors)
    low, high = edge_rows(parents)
    place = lax.axis_index("lat").astype(jnp.int32)[None]
    result = stencil(place, parents, low, high, forcing, force_low, force_high)
    return result.reshape(ensemble.shape)


def solution(mesh):
    placed = (
        P(("groups", "mem"), None, "lat", None),
        P(None, "lat", None),
        P("groups"),
        P(("groups", "mem")),
    )
    return jax.shard_map(
        on_device,
        mesh=mesh,
        in_specs=placed,
        out_specs=P(("groups", "mem"), None, "lat", None),
        check_vma=False,
    )
```

```python
import functools

import jax
import jax.numpy as jnp
from jax import lax
from jax.experimental import pallas as pl
from jax.experimental.pallas import tpu as pltpu
from jax.sharding import PartitionSpec as P

STEPS = 3


TIME_STEP = 0.25
DENSITY_RATIO = 0.9
DRAG_RATE = 0.1
CORIOLIS_MEAN = 0.5

TILE = 8
LANES = 128


HEIGHT_SCALE = TIME_STEP * TIME_STEP / 2
SPEED_SCALE = TIME_STEP / 2


def stencil_kernel(count, pieces, place_ref, starts_ref, *refs):
    parent_refs = refs[:pieces]
    low_ref, high_ref, force_ref, force_low_ref, force_high_ref, out_ref, first, second, force = refs[pieces:]
    rows, columns = force_ref.shape
    blocks = rows // TILE
    strips = columns // LANES
    place = place_ref[0]
    total = float(rows * count)
    tile = (TILE, LANES)
    sub = lax.broadcasted_iota(jnp.int32, tile, 0)
    lane = lax.broadcasted_iota(jnp.int32, tile, 1)
    bottom = sub == 0
    left = lane == 0
    right = lane == LANES - 1
    zero = jnp.zeros(tile, jnp.float32)
    head = 2 * TILE
    last = head + rows

    def scaled(field, value):
        return HEIGHT_SCALE + HEIGHT_SCALE * value if field % 3 == 0 else SPEED_SCALE * value

    for strip in range(strips):
        span = slice(strip * LANES, (strip + 1) * LANES)
        for field in range(6):
            low = scaled(field, jnp.where(place > 0, low_ref[field, :, span], 0.0))
            high = scaled(field, jnp.where(place < count - 1, high_ref[field, :, span], 0.0))
            for buffer in (first, second):
                buffer[field, strip, :TILE] = zero
                buffer[field, strip, last + TILE : last + 2 * TILE] = zero
                buffer[field, strip, last + 2 * TILE :] = zero
                buffer[field, strip, TILE:head] = low
                buffer[field, strip, last : last + TILE] = high
            for piece, parent_ref in enumerate(parent_refs):
                height = parent_ref.shape[1]
                here = pl.ds(pl.multiple_of(head + starts_ref[piece], TILE), height)
                first[field, strip, here] = scaled(field, parent_ref[field, :, span])
            if field % 3 == 2:
                edge = first[field, strip, head : head + TILE]
                first[field, strip, head : head + TILE] = jnp.where(sub + place > 0, edge, 0.0)
        force[strip, TILE:head] = (TIME_STEP * SPEED_SCALE) * force_low_ref[:, span]
        force[strip, head:last] = (TIME_STEP * SPEED_SCALE) * force_ref[:, span]
        force[strip, last : last + TILE] = (TIME_STEP * SPEED_SCALE) * force_high_ref[:, span]

    def west(values):
        turned = [pltpu.roll(value, 1, 1) for value in values]
        return [jnp.where(left, turned[i - 1], turned[i]) for i in range(strips)]

    def east(values):
        turned = [pltpu.roll(value, LANES - 1, 1) for value in values]
        return [jnp.where(right, turned[(i + 1) % strips], turned[i]) for i in range(strips)]

    def load(source, field, block, offset=0):
        return [source[field, strip, pl.ds(TILE * (block + 1) + offset, TILE)] for strip in range(strips)]

    def each(function, *lists):
        return [function(*items) for items in zip(*lists)]

    def keep(target, field, block, values):
        for strip in range(strips):
            target[field, strip, pl.ds(pl.multiple_of(TILE * (block + 1), TILE), TILE)] = values[strip]

    def give(field, block, values):
        for strip in range(strips):
            value = values[strip] * (1.0 / HEIGHT_SCALE) - 1.0 if field % 3 == 0 else values[strip] * (1.0 / SPEED_SCALE)
            out_ref[field, pl.ds(pl.multiple_of(TILE * (block - 1), TILE), TILE), strip * LANES : (strip + 1) * LANES] = value

    def heights(source, target, block):
        for base in (0, 3):
            thick = load(source, base, block)
            flux_x = each(lambda u, t, w: u * (t + w), load(source, base + 1, block), thick, west(thick))
            flux_y = each(lambda v, t, b: v * (t + b), load(source, base + 2, block), thick, load(source, base, block, -1))
            above_flux = each(lambda v, t, a: v * (t + a), load(source, base + 2, block, 1), thick, load(source, base, block, 1))
            new = each(lambda h, e, x, a, y: (h - (e - x)) - (a - y), thick, east(flux_x), flux_x, above_flux, flux_y)
            keep(target, base, block, new)

    def speeds(source, target, block, store):
        row = (sub + ((block - 1) * TILE + place * rows)).astype(jnp.float32)
        coriolis_u = (0.25 * TIME_STEP) * (CORIOLIS_MEAN + (row * (1.0 / total) - 0.5))
        coriolis_v = (0.25 * TIME_STEP) * (CORIOLIS_MEAN + ((row - 0.5) * (1.0 / total) - 0.5))
        upper, lower = load(target, 0, block), load(target, 3, block)
        below_upper, below_lower = load(target, 0, block, -1), load(target, 3, block, -1)
        for layer in range(2):
            base = 3 * layer
            if layer == 0:
                pressure = each(lambda a, b: a + b, upper, lower)
                below_pressure = each(lambda a, b: a + b, below_upper, below_lower)
            else:
                pressure = each(lambda a, b: DENSITY_RATIO * a + b, upper, lower)
                below_pressure = each(lambda a, b: DENSITY_RATIO * a + b, below_upper, below_lower)
            speed_u = load(source, base + 1, block)
            speed_v = load(source, base + 2, block)
            turn_v = each(lambda v, a: coriolis_u * (v + a), speed_v, load(source, base + 2, block, 1))
            if layer == 0:
                forced = [speed_u[strip] + force[strip, pl.ds(pl.multiple_of(TILE * (block + 1), TILE), TILE)] for strip in range(strips)]
            else:
                forced = [(1.0 - TIME_STEP * DRAG_RATE) * value for value in speed_u]
            pushed = west(each(lambda t, p: t + p, turn_v, pressure))
            store(base + 1, block, each(lambda f, t, p, w: (f + (t - p)) + w, forced, turn_v, pressure, pushed))
            sum_u = each(lambda u, b: u + b, speed_u, load(source, base + 1, block, -1))
            slope = each(lambda p, b: p - b, pressure, below_pressure)
            store(base + 2, block, each(lambda v, s, es, d: (v - coriolis_v * (s + es)) - d, speed_v, sum_u, east(sum_u), slope))

    start = jnp.where(place == 0, 1, 0)
    stop = jnp.where(place == count - 1, blocks + 1, blocks + 2)
    source, target = first, second
    for _ in range(STEPS - 1):
        heights(source, target, start)

        def step(block, carry, source=source, target=target):
            heights(source, target, block + 1)
            speeds(source, target, block, functools.partial(keep, target))
            return carry

        lax.fori_loop(start, stop, step, 0)

        @pl.when(place == 0)
        def _():
            for field in (2, 5):
                for strip in range(strips):
                    target[field, strip, head : head + TILE] = jnp.where(bottom, 0.0, target[field, strip, head : head + TILE])

        source, target = target, source
    heights(source, target, 0)
    heights(source, target, 1)

    def finish(block, carry):
        heights(source, target, block + 1)
        give(0, block, load(target, 0, block))
        give(3, block, load(target, 3, block))
        speeds(source, target, block, give)
        return carry

    lax.fori_loop(1, blocks + 1, finish, 0)

    @pl.when(place == 0)
    def _():
        for field in (2, 5):
            for strip in range(strips):
                span = slice(strip * LANES, (strip + 1) * LANES)
                out_ref[field, :TILE, span] = jnp.where(bottom, 0.0, out_ref[field, :TILE, span])


def stencil(parents, starts, edges, forcing, force_edges):
    rows, columns = forcing.shape
    fields_count = parents[0].shape[0]
    shape = (fields_count, columns // LANES, rows + 5 * TILE, LANES)
    vmem = pl.BlockSpec(memory_space=pltpu.VMEM)
    smem = pl.BlockSpec(memory_space=pltpu.SMEM)
    place = lax.axis_index("lat").astype(jnp.int32)[None]
    return pl.pallas_call(
        functools.partial(stencil_kernel, lax.axis_size("lat"), len(parents)),
        out_shape=jax.ShapeDtypeStruct((fields_count, rows, columns), jnp.float32),
        in_specs=[smem] * 2 + [vmem] * (len(parents) + 5),
        out_specs=vmem,
        scratch_shapes=[pltpu.VMEM(shape, jnp.float32), pltpu.VMEM(shape, jnp.float32), pltpu.VMEM(shape[1:], jnp.float32)],
        compiler_params=pltpu.CompilerParams(vmem_limit_bytes=12 << 20),
        cost_estimate=pl.CostEstimate(flops=300 * rows * columns, bytes_accessed=52 * rows * columns, transcendentals=0),
    )(place, starts, *parents, *edges, forcing, *force_edges)


def edge_rows(block):
    rows = block.shape[-2]
    dim = block.ndim - 2
    count = lax.axis_size("lat")
    if count == 2:
        sent = lax.dynamic_slice_in_dim(block, (1 - lax.axis_index("lat")) * (rows - TILE), TILE, axis=dim)
        return swap_edges(sent)
    forward = [(i, i + 1) for i in range(count - 1)]
    backward = [(target, source) for source, target in forward]
    below = lax.ppermute(lax.slice_in_dim(block, rows - TILE, rows, axis=dim), "lat", forward)
    above = lax.ppermute(lax.slice_in_dim(block, 0, TILE, axis=dim), "lat", backward)
    return below, above


def swap_edges(sent):
    got = lax.ppermute(sent, "lat", [(0, 1), (1, 0)])
    return got, got


def by_all_to_all(block, ancestors):
    fields_count, band_rows, columns = block.shape
    count = lax.axis_size("mem")
    pieces = block.reshape(count, fields_count * band_rows // count, columns)
    spread = lax.all_to_all(pieces, "mem", split_axis=0, concat_axis=0, tiled=True)
    taken = jnp.take(spread, ancestors, axis=0, mode="clip")
    moved = lax.all_to_all(taken, "mem", split_axis=0, concat_axis=0, tiled=True)
    return moved.reshape(block.shape)


PARTS = 4
MEMBERS = 2 * PARTS
CHUNKS = 2


def shift(values, distance):
    return lax.ppermute(values, "mem", [(i, i ^ distance) for i in range(MEMBERS)])


def small_call(kernel, count, shape, scalars, arrays, held, scratch=()):
    vmem = pl.BlockSpec(memory_space=pltpu.VMEM)
    size = 4 * shape[0] * shape[1] * shape[2]
    return pl.pallas_call(
        kernel,
        out_shape=[jax.ShapeDtypeStruct(shape, jnp.float32)] * count,
        in_specs=[pl.BlockSpec(memory_space=pltpu.SMEM)] + [vmem] * held + [pl.BlockSpec(memory_space=pl.ANY)] * (len(arrays) - held),
        out_specs=[vmem] * count,
        scratch_shapes=list(scratch),
        compiler_params=pltpu.CompilerParams(vmem_limit_bytes=4 << 20),
        cost_estimate=pl.CostEstimate(flops=0, bytes_accessed=2 * count * size, transcendentals=0),
    )(scalars, *arrays)


def cut_kernel(starts_ref, block_ref, *refs):
    outs, sem = refs[-PARTS - 1 : -1], refs[-1]
    height = outs[0].shape[1]
    copies = []
    for k, out in enumerate(outs):
        rows = pl.ds(pl.multiple_of(starts_ref[k], TILE), height)
        copies.append(pltpu.make_async_copy(block_ref.at[:, rows, :], out, sem.at[k]))
    for copy in copies:
        copy.start()
    for copy in copies:
        copy.wait()


def cut(block, starts, height, after):
    shape = (block.shape[0], height, block.shape[2])
    return small_call(cut_kernel, PARTS, shape, starts, [block, *after], 0, [pltpu.SemaphoreType.DMA((PARTS,))])


def route_kernel(sources, count, chosen_ref, *refs):
    for k, out in enumerate(refs[-count:]):
        for j, source in enumerate(refs[:sources]):

            @pl.when(chosen_ref[k] == j)
            def _():
                out[...] = source[...]


def route(chosen, sources, count, after=()):
    kernel = functools.partial(route_kernel, len(sources), count)
    return small_call(kernel, count, sources[0].shape, chosen, [*sources, *after], len(sources))


def edge_kernel(chosen_ref, *refs):
    out = refs[-1]
    for j, source in enumerate(refs[:-1]):

        @pl.when(chosen_ref[0] == j)
        def _():
            out[...] = source[:, pl.ds(pl.multiple_of(chosen_ref[1], TILE), TILE), :]


def crossings(ancestors):
    ids = jnp.arange(MEMBERS, dtype=jnp.int32)
    far = ids[:, None] // PARTS != ids[None, :] // PARTS
    need = jnp.any((ancestors[:, None] == ids[None, :]) & far, axis=0)
    ahead = need[:, None] & (ids[:, None] < ids[None, :]) & ~far
    return need, jnp.sum(ahead.astype(jnp.int32), axis=0)


def by_crossings(block, ancestors, finish):
    fields_count, rows, columns = block.shape
    ids = jnp.arange(MEMBERS, dtype=jnp.int32)
    member = lax.axis_index("mem").astype(jnp.int32)
    half, own = member // PARTS, member % PARTS
    parts = own ^ jnp.arange(PARTS, dtype=jnp.int32)
    span = rows // CHUNKS
    height = span // PARTS
    near = (lax.axis_index("lat") == 0).astype(jnp.int32)
    starts = [((CHUNKS - 1 - c) * near + c * (1 - near)) * span + parts * height for c in range(CHUNKS)]

    def spread(c, block, after):
        held = cut(block, starts[c], height, after)
        return [held[0]] + [shift(held[k], k) for k in range(1, PARTS)]

    need, rank = crossings(ancestors)
    most = jnp.max(rank + need.astype(jnp.int32))[None]
    groups = lax.axis_size("groups")
    for distance in range(1, groups):
        other = lax.ppermute(most, "groups", [(i, (i + distance) % groups) for i in range(groups)])
        most = jnp.maximum(most, other)
    slots = half * PARTS + parts
    parent = jnp.sum(jnp.where(slots[:, None] == ids[None, :], ancestors[None, :], 0), axis=1)
    parent_rank = jnp.sum(jnp.where(parent[:, None] == ids[None, :], rank[None, :], 0), axis=1)
    given_index = jnp.where(parent // PARTS == half, (parent % PARTS) ^ own, PARTS + parent_rank)

    def plan(rounds, block, shared, need, rank, given_index, rest):
        turns = jnp.arange(rounds, dtype=jnp.int32)
        mine = need & (ids // PARTS == half)
        order = jnp.sum(jnp.where(mine[None, :] & (rank[None, :] == turns[:, None]), ids[None, :] % PARTS, 0), axis=1)
        crossed, final = (), []
        for c in range(CHUNKS):
            if c > 0:
                shared = spread(c, block, shared[1:])
            sent = route(order ^ own, shared, rounds, crossed)
            crossed = [shift(part, PARTS) for part in sent]
            given = route(given_index, [*shared, *crossed], PARTS)
            final.append([given[0]] + [shift(given[k], k) for k in range(1, PARTS)])
        return finish(final, starts, *rest)

    return spread(0, block, ()), most, (need, rank, given_index), plan


def on_device(ensemble, forcing_table, ancestors, selector):
    rows = ensemble.shape[2]
    block = ensemble.reshape(ensemble.shape[1:])
    forcing = lax.dynamic_index_in_dim(forcing_table, selector[0], 0, keepdims=False)
    force_edges = edge_rows(forcing)
    fits = lax.axis_size("mem") == MEMBERS and lax.axis_size("lat") == 2 and rows % (CHUNKS * PARTS * TILE) == 0
    if not fits:
        parents = by_all_to_all(block, ancestors)
        result = stencil([parents], jnp.zeros(1, jnp.int32), edge_rows(parents), forcing, force_edges)
        return result.reshape(ensemble.shape)

    def finish(final, starts, forcing, below, above):
        height = final[0][0].shape[1]
        own = lax.axis_index("mem").astype(jnp.int32) % PARTS
        near = (lax.axis_index("lat") == 0).astype(jnp.int32)
        chosen = jnp.stack([own ^ ((PARTS - 1) * near), (height - TILE) * near])
        edge = small_call(edge_kernel, 1, (block.shape[0], TILE, block.shape[2]), chosen, final[0], PARTS)[0]
        pieces = [piece for chunk in final for piece in chunk]
        return stencil(pieces, jnp.concatenate(starts), swap_edges(edge), forcing, (below, above))

    shared, most, tables, plan = by_crossings(block, ancestors, finish)
    branches = [functools.partial(plan, rounds) for rounds in range(2, PARTS + 1)]
    choice = jnp.clip(most[0] - 2, 0, PARTS - 2)
    result = lax.switch(choice, branches, block, shared, *tables, (forcing, *force_edges))
    return result.reshape(ensemble.shape)


def solution(mesh):
    placed = (
        P(("groups", "mem"), None, "lat", None),
        P(None, "lat", None),
        P("groups"),
        P(("groups", "mem")),
    )
    return jax.shard_map(
        on_device,
        mesh=mesh,
        in_specs=placed,
        out_specs=P(("groups", "mem"), None, "lat", None),
        check_vma=False,
    )
```

```python
import functools

import jax
import jax.numpy as jnp
from jax import lax
from jax.experimental import pallas as pl
from jax.experimental.pallas import tpu as pltpu
from jax.sharding import PartitionSpec as P

STEPS = 3


TIME_STEP = 0.25
DENSITY_RATIO = 0.9
DRAG_RATE = 0.1
CORIOLIS_MEAN = 0.5

TILE = 8
LANES = 128
SLABS = 4


HEIGHT_SCALE = TIME_STEP * TIME_STEP / 2
SPEED_SCALE = TIME_STEP / 2


def stencil_kernel(count, chunks, pieces, here_ref, *refs):
    parent_refs = refs[:pieces]
    low_ref, high_ref, force_ref, force_low_ref, force_high_ref, out_ref, first, second, force, result, sem = refs[pieces:]
    rows, columns = force_ref.shape
    blocks = rows // TILE
    strips = columns // LANES
    place = here_ref[1]
    total = float(rows * count)
    tile = (TILE, LANES)
    sub = lax.broadcasted_iota(jnp.int32, tile, 0)
    lane = lax.broadcasted_iota(jnp.int32, tile, 1)
    bottom = sub == 0
    left = lane == 0
    right = lane == LANES - 1
    zero = jnp.zeros(tile, jnp.float32)
    head = 2 * TILE
    last = head + rows

    def scaled(field, value):
        return HEIGHT_SCALE + HEIGHT_SCALE * value if field % 3 == 0 else SPEED_SCALE * value

    for strip in range(strips):
        span = slice(strip * LANES, (strip + 1) * LANES)
        for field in range(6):
            low = scaled(field, jnp.where(place > 0, low_ref[field, :, span], 0.0))
            high = scaled(field, jnp.where(place < count - 1, high_ref[field, :, span], 0.0))
            for buffer in (first, second):
                buffer[field, strip, :TILE] = zero
                buffer[field, strip, last + TILE : last + 2 * TILE] = zero
                buffer[field, strip, last + 2 * TILE :] = zero
                buffer[field, strip, TILE:head] = low
                buffer[field, strip, last : last + TILE] = high
            for piece, parent_ref in enumerate(parent_refs):
                height = parent_ref.shape[1]
                first_row = head if pieces == 1 else head + part_start(here_ref, chunks[piece // PARTS], piece % PARTS, rows)
                span_rows = pl.ds(pl.multiple_of(first_row, TILE), height)
                first[field, strip, span_rows] = scaled(field, parent_ref[field, :, span])
            if field % 3 == 2:
                edge = first[field, strip, head : head + TILE]
                first[field, strip, head : head + TILE] = jnp.where(sub + place > 0, edge, 0.0)
        force[strip, TILE:head] = (TIME_STEP * SPEED_SCALE) * force_low_ref[:, span]
        force[strip, head:last] = (TIME_STEP * SPEED_SCALE) * force_ref[:, span]
        force[strip, last : last + TILE] = (TIME_STEP * SPEED_SCALE) * force_high_ref[:, span]

    def west(values):
        turned = [pltpu.roll(value, 1, 1) for value in values]
        return [jnp.where(left, turned[i - 1], turned[i]) for i in range(strips)]

    def east(values):
        turned = [pltpu.roll(value, LANES - 1, 1) for value in values]
        return [jnp.where(right, turned[(i + 1) % strips], turned[i]) for i in range(strips)]

    def load(source, field, block, offset=0):
        return [source[field, strip, pl.ds(TILE * (block + 1) + offset, TILE)] for strip in range(strips)]

    def each(function, *lists):
        return [function(*items) for items in zip(*lists)]

    def keep(target, field, block, values):
        for strip in range(strips):
            target[field, strip, pl.ds(pl.multiple_of(TILE * (block + 1), TILE), TILE)] = values[strip]

    def give(field, block, values):
        for strip in range(strips):
            value = values[strip] * (1.0 / HEIGHT_SCALE) - 1.0 if field % 3 == 0 else values[strip] * (1.0 / SPEED_SCALE)
            result[field, pl.ds(pl.multiple_of(TILE * (block - 1), TILE), TILE), strip * LANES : (strip + 1) * LANES] = value

    def heights(source, target, block):
        for base in (0, 3):
            thick = load(source, base, block)
            flux_x = each(lambda u, t, w: u * (t + w), load(source, base + 1, block), thick, west(thick))
            flux_y = each(lambda v, t, b: v * (t + b), load(source, base + 2, block), thick, load(source, base, block, -1))
            above_flux = each(lambda v, t, a: v * (t + a), load(source, base + 2, block, 1), thick, load(source, base, block, 1))
            new = each(lambda h, e, x, a, y: (h - (e - x)) - (a - y), thick, east(flux_x), flux_x, above_flux, flux_y)
            keep(target, base, block, new)

    def speeds(source, target, block, store):
        row = (sub + ((block - 1) * TILE + place * rows)).astype(jnp.float32)
        coriolis_u = (0.25 * TIME_STEP) * (CORIOLIS_MEAN + (row * (1.0 / total) - 0.5))
        coriolis_v = (0.25 * TIME_STEP) * (CORIOLIS_MEAN + ((row - 0.5) * (1.0 / total) - 0.5))
        upper, lower = load(target, 0, block), load(target, 3, block)
        below_upper, below_lower = load(target, 0, block, -1), load(target, 3, block, -1)
        for layer in range(2):
            base = 3 * layer
            if layer == 0:
                pressure = each(lambda a, b: a + b, upper, lower)
                below_pressure = each(lambda a, b: a + b, below_upper, below_lower)
            else:
                pressure = each(lambda a, b: DENSITY_RATIO * a + b, upper, lower)
                below_pressure = each(lambda a, b: DENSITY_RATIO * a + b, below_upper, below_lower)
            speed_u = load(source, base + 1, block)
            speed_v = load(source, base + 2, block)
            turn_v = each(lambda v, a: coriolis_u * (v + a), speed_v, load(source, base + 2, block, 1))
            if layer == 0:
                forced = [speed_u[strip] + force[strip, pl.ds(pl.multiple_of(TILE * (block + 1), TILE), TILE)] for strip in range(strips)]
            else:
                forced = [(1.0 - TIME_STEP * DRAG_RATE) * value for value in speed_u]
            pushed = west(each(lambda t, p: t + p, turn_v, pressure))
            store(base + 1, block, each(lambda f, t, p, w: (f + (t - p)) + w, forced, turn_v, pressure, pushed))
            sum_u = each(lambda u, b: u + b, speed_u, load(source, base + 1, block, -1))
            slope = each(lambda p, b: p - b, pressure, below_pressure)
            store(base + 2, block, each(lambda v, s, es, d: (v - coriolis_v * (s + es)) - d, speed_v, sum_u, east(sum_u), slope))

    start = jnp.where(place == 0, 1, 0)
    stop = jnp.where(place == count - 1, blocks + 1, blocks + 2)
    source, target = first, second
    for _ in range(STEPS - 1):
        heights(source, target, start)

        def step(block, carry, source=source, target=target):
            heights(source, target, block + 1)
            speeds(source, target, block, functools.partial(keep, target))
            return carry

        lax.fori_loop(start, stop, step, 0)

        @pl.when(place == 0)
        def _():
            for field in (2, 5):
                for strip in range(strips):
                    target[field, strip, head : head + TILE] = jnp.where(bottom, 0.0, target[field, strip, head : head + TILE])

        source, target = target, source
    heights(source, target, 0)
    heights(source, target, 1)

    def finish(block, carry):
        heights(source, target, block + 1)
        give(0, block, load(target, 0, block))
        give(3, block, load(target, 3, block))
        speeds(source, target, block, give)
        return carry

    copies = []
    for part in range(SLABS):
        first_block, end_block = part * blocks // SLABS, (part + 1) * blocks // SLABS
        lax.fori_loop(first_block + 1, end_block + 1, finish, 0)
        if part == 0:

            @pl.when(place == 0)
            def _():
                for field in (2, 5):
                    for strip in range(strips):
                        span = slice(strip * LANES, (strip + 1) * LANES)
                        result[field, :TILE, span] = jnp.where(bottom, 0.0, result[field, :TILE, span])

        slab = slice(TILE * first_block, TILE * end_block)
        copies.append(pltpu.make_async_copy(result.at[:, slab, :], out_ref.at[:, slab, :], sem.at[part]))
        copies[-1].start()
    for copy in copies:
        copy.wait()


def stencil(here, parents, edges, forcing, force_edges):
    rows, columns = forcing.shape
    fields_count = parents[0].shape[0]
    shape = (fields_count, columns // LANES, rows + 5 * TILE, LANES)
    vmem = pl.BlockSpec(memory_space=pltpu.VMEM)
    smem = pl.BlockSpec(memory_space=pltpu.SMEM)
    return pl.pallas_call(
        functools.partial(stencil_kernel, lax.axis_size("lat"), chunks_of(rows), len(parents)),
        out_shape=jax.ShapeDtypeStruct((fields_count, rows, columns), jnp.float32),
        in_specs=[smem] + [vmem] * (len(parents) + 5),
        out_specs=pl.BlockSpec(memory_space=pltpu.HBM),
        scratch_shapes=[
            pltpu.VMEM(shape, jnp.float32),
            pltpu.VMEM(shape, jnp.float32),
            pltpu.VMEM(shape[1:], jnp.float32),
            pltpu.VMEM((fields_count, rows, columns), jnp.float32),
            pltpu.SemaphoreType.DMA((SLABS,)),
        ],
        compiler_params=pltpu.CompilerParams(vmem_limit_bytes=12 << 20),
        cost_estimate=pl.CostEstimate(flops=300 * rows * columns, bytes_accessed=52 * rows * columns, transcendentals=0),
    )(here, *parents, *edges, forcing, *force_edges)


def edge_rows(block):
    rows = block.shape[-2]
    dim = block.ndim - 2
    count = lax.axis_size("lat")
    if count == 2:
        sent = lax.dynamic_slice_in_dim(block, (1 - lax.axis_index("lat")) * (rows - TILE), TILE, axis=dim)
        return swap_edges(sent)
    forward = [(i, i + 1) for i in range(count - 1)]
    backward = [(target, source) for source, target in forward]
    below = lax.ppermute(lax.slice_in_dim(block, rows - TILE, rows, axis=dim), "lat", forward)
    above = lax.ppermute(lax.slice_in_dim(block, 0, TILE, axis=dim), "lat", backward)
    return below, above


def swap_edges(sent):
    got = lax.ppermute(sent, "lat", [(0, 1), (1, 0)])
    return got, got


def by_all_to_all(block, ancestors):
    fields_count, band_rows, columns = block.shape
    count = lax.axis_size("mem")
    pieces = block.reshape(count, fields_count * band_rows // count, columns)
    spread = lax.all_to_all(pieces, "mem", split_axis=0, concat_axis=0, tiled=True)
    taken = jnp.take(spread, ancestors, axis=0, mode="clip")
    moved = lax.all_to_all(taken, "mem", split_axis=0, concat_axis=0, tiled=True)
    return moved.reshape(block.shape)


PARTS = 4
MEMBERS = 2 * PARTS
CHUNKS = (1, 1)


def chunks_of(rows):
    spans = [rows * share // sum(CHUNKS) for share in CHUNKS]
    return [(sum(spans[:c]), span) for c, span in enumerate(spans)]


def part_start(here_ref, chunk, k, rows):
    passed, span = chunk
    own = lax.rem(here_ref[0], PARTS)
    return jnp.where(here_ref[1] == 0, rows - passed - span, passed) + (own ^ k) * (span // PARTS)


def shift(values, distance):
    return lax.ppermute(values, "mem", [(i, i ^ distance) for i in range(MEMBERS)])


def small_call(kernel, outs, here, tables, arrays, left, scratch=()):
    vmem = pl.BlockSpec(memory_space=pltpu.VMEM)
    smem = pl.BlockSpec(memory_space=pltpu.SMEM)
    anywhere = pl.BlockSpec(memory_space=pl.ANY)
    moved = sum(2 * out.size * 4 for out in outs)
    return pl.pallas_call(
        kernel,
        out_shape=outs,
        in_specs=[smem] * (1 + len(tables)) + [vmem] * len(arrays) + [anywhere] * len(left),
        out_specs=[vmem if out.ndim > 1 else smem for out in outs],
        scratch_shapes=list(scratch),
        compiler_params=pltpu.CompilerParams(vmem_limit_bytes=4 << 20),
        cost_estimate=pl.CostEstimate(flops=0, bytes_accessed=moved, transcendentals=0),
    )(here, *tables, *arrays, *left)


def part_shape(block, chunk):
    return jax.ShapeDtypeStruct((block.shape[0], chunk[1] // PARTS, block.shape[2]), jnp.float32)


def cut_kernel(chunk, here_ref, block_ref, *refs):
    outs, sem = refs[-PARTS:-1], refs[-1]
    copies = []
    for k, out in enumerate(outs):
        first_row = part_start(here_ref, chunk, k + 1, block_ref.shape[1])
        rows = pl.ds(pl.multiple_of(first_row, TILE), out.shape[1])
        copies.append(pltpu.make_async_copy(block_ref.at[:, rows, :], out, sem.at[k]))
    for copy in copies:
        copy.start()
    for copy in copies:
        copy.wait()


def cut(here, block, chunk, after):
    outs = [part_shape(block, chunk)] * (PARTS - 1)
    kernel = functools.partial(cut_kernel, chunk)
    return small_call(kernel, outs, here, [], [], [block, *after], [pltpu.SemaphoreType.DMA((PARTS - 1,))])


def route_kernel(chunk, sources, count, here_ref, chosen_ref, *refs):
    source_refs, block_ref = refs[:sources], refs[sources]
    outs, sem = refs[-count - 1 : -1], refs[-1]
    first_row = part_start(here_ref, chunk, 0, block_ref.shape[1])
    rows = pl.ds(pl.multiple_of(first_row, TILE), outs[0].shape[1])
    copies = [pltpu.make_async_copy(block_ref.at[:, rows, :], out, sem.at[k]) for k, out in enumerate(outs)]
    for k, copy in enumerate(copies):
        pl.when(chosen_ref[k] == 0)(copy.start)
    for k, out in enumerate(outs):
        for j, source in enumerate(source_refs):

            @pl.when(chosen_ref[k] == j + 1)
            def _():
                out[...] = source[...]

    for k, copy in enumerate(copies):
        pl.when(chosen_ref[k] == 0)(copy.wait)


def route(here, chosen, count, block, chunk, sources, after=()):
    outs = [part_shape(block, chunk)] * count
    kernel = functools.partial(route_kernel, chunk, len(sources), count)
    return small_call(kernel, outs, here, [chosen], sources, [block, *after], [pltpu.SemaphoreType.DMA((count,))])


def edge_kernel(here_ref, *refs):
    out = refs[-1]
    own = lax.rem(here_ref[0], PARTS)
    rows = refs[0].shape[1]
    for k, source in enumerate(refs[:PARTS]):
        for place, owner, first_row in ((0, PARTS - 1, rows - TILE), (1, 0, 0)):

            @pl.when((here_ref[1] == place) & ((own ^ k) == owner))
            def _():
                out[...] = source[:, first_row : first_row + TILE, :]


def tables_kernel(here_ref, ancestors_ref, *refs):
    order_ref, given_ref, most_ref, rank_ref = refs[-4:]
    member = here_ref[0]
    half, own = member // PARTS, lax.rem(member, PARTS)
    for r in range(PARTS):
        order_ref[r] = 0
    most = 0
    for side in range(2):
        rank = 0
        for place in range(PARTS):
            p = side * PARTS + place
            need = 0
            for slot in range((1 - side) * PARTS, (2 - side) * PARTS):
                need = need | jnp.where(ancestors_ref[slot] == p, 1, 0)
            rank_ref[p] = rank

            @pl.when((need > 0) & (half == side))
            def _():
                order_ref[rank] = own ^ place

            rank = rank + need
        most = jnp.maximum(most, rank)
    most_ref[0] = most
    for k in range(PARTS):
        parent = ancestors_ref[half * PARTS + (own ^ k)]
        given_ref[k] = jnp.where(parent // PARTS == half, lax.rem(parent, PARTS) ^ own, PARTS + rank_ref[parent])


def tables_of(here, ancestors, after):
    outs = [jax.ShapeDtypeStruct((size,), jnp.int32) for size in (PARTS, PARTS, 1)]
    return small_call(tables_kernel, outs, here, [ancestors], [], after, [pltpu.SMEM((MEMBERS,), jnp.int32)])


def by_crossings(here, block, ancestors):
    chunks = chunks_of(block.shape[1])

    def spread(held):
        return [shift(part, k + 1) for k, part in enumerate(held)]

    held = cut(here, block, chunks[0], ())
    shared = spread(held)
    order, given_index, most = tables_of(here, ancestors, held[:1])
    groups = lax.axis_size("groups")
    other = most
    for _ in range(groups - 1):
        other = lax.ppermute(other, "groups", [(i, (i + 1) % groups) for i in range(groups)])
        most = jnp.maximum(most, other)

    def plan(rounds, here, block, shared, order, given_index):
        crossed, final = (), []
        for c, chunk in enumerate(chunks):
            sent = route(here, order, rounds, block, chunk, shared, crossed[:1])
            following = ()
            if c + 1 < len(chunks):
                following = spread(cut(here, block, chunks[c + 1], (*shared, sent[0])))
            crossed = [shift(part, PARTS) for part in sent]
            given = route(here, given_index, PARTS, block, chunk, [*shared, *crossed])
            final.append([given[0]] + [shift(given[k], k) for k in range(1, PARTS)])
            shared = following
        edge_shape = jax.ShapeDtypeStruct((block.shape[0], TILE, block.shape[2]), jnp.float32)
        edge = small_call(edge_kernel, [edge_shape], here, [], final[0], [])[0]
        return [part for parts in final for part in parts], swap_edges(edge)[0]

    branches = [functools.partial(plan, rounds) for rounds in range(2, PARTS + 1)]
    return lax.switch(jnp.clip(most[0] - 2, 0, PARTS - 2), branches, here, block, shared, order, given_index)


def on_device(ensemble, forcing_table, ancestors, selector):
    rows = ensemble.shape[2]
    block = ensemble.reshape(ensemble.shape[1:])
    here = jnp.stack([lax.axis_index("mem"), lax.axis_index("lat")]).astype(jnp.int32)
    forcing = lax.dynamic_index_in_dim(forcing_table, selector[0], 0, keepdims=False)
    force_edges = edge_rows(forcing)
    if lax.axis_size("mem") == MEMBERS and lax.axis_size("lat") == 2 and rows % (sum(CHUNKS) * PARTS * TILE) == 0:
        parents, edge = by_crossings(here, block, ancestors)
        edges = (edge, edge)
    else:
        parents = [by_all_to_all(block, ancestors)]
        edges = edge_rows(parents[0])
    return stencil(here, parents, edges, forcing, force_edges).reshape(ensemble.shape)


def solution(mesh):
    placed = (
        P(("groups", "mem"), None, "lat", None),
        P(None, "lat", None),
        P("groups"),
        P(("groups", "mem")),
    )
    return jax.shard_map(
        on_device,
        mesh=mesh,
        in_specs=placed,
        out_specs=P(("groups", "mem"), None, "lat", None),
        check_vma=False,
    )
```

```python
import functools

import jax
import jax.numpy as jnp
from jax import lax
from jax.experimental import pallas as pl
from jax.experimental.pallas import tpu as pltpu
from jax.sharding import PartitionSpec as P

STEPS = 3


TIME_STEP = 0.25
DENSITY_RATIO = 0.9
DRAG_RATE = 0.1
CORIOLIS_MEAN = 0.5

TILE = 8
LANES = 128
SLABS = 2
GROUP = 4
MARGIN = 5


HEIGHT_SCALE = TIME_STEP * TIME_STEP / 2
SPEED_SCALE = TIME_STEP / 2


def stencil_kernel(count, chunks, pieces, here_ref, *refs):
    parent_refs = refs[:pieces]
    low_ref, high_ref, force_ref, force_low_ref, force_high_ref, out_ref = refs[pieces : pieces + 6]
    first, second, force, shifted, spread, result, sem = refs[pieces + 6 :]
    rows, columns = force_ref.shape
    blocks = rows // TILE
    strips = columns // LANES
    place = here_ref[1]
    total = float(rows * count)
    tile = (TILE, LANES)
    sub = lax.broadcasted_iota(jnp.int32, tile, 0)
    lane = lax.broadcasted_iota(jnp.int32, tile, 1)
    bottom = sub == 0
    left = lane == 0
    right = lane == LANES - 1
    head = MARGIN * TILE
    last = head + rows

    def scaled(field, value):
        return HEIGHT_SCALE + HEIGHT_SCALE * value if field % 3 == 0 else SPEED_SCALE * value

    for strip in range(strips):
        span = slice(strip * LANES, (strip + 1) * LANES)
        for field in range(6):
            low = scaled(field, jnp.where(place > 0, low_ref[field, :, span], 0.0))
            high = scaled(field, jnp.where(place < count - 1, high_ref[field, :, span], 0.0))
            for buffer in (first, second):
                buffer[field, strip, : head - TILE] = jnp.zeros((head - TILE, LANES), jnp.float32)
                buffer[field, strip, last + TILE :] = jnp.zeros((head - TILE, LANES), jnp.float32)
                buffer[field, strip, head - TILE : head] = low
                buffer[field, strip, last : last + TILE] = high
            for piece, parent_ref in enumerate(parent_refs):
                height = parent_ref.shape[1]
                first_row = head if pieces == 1 else head + part_start(here_ref, chunks[piece // PARTS], piece % PARTS, rows)
                span_rows = pl.ds(pl.multiple_of(first_row, TILE), height)
                first[field, strip, span_rows] = scaled(field, parent_ref[field, :, span])
            if field % 3 == 2:
                edge = first[field, strip, head : head + TILE]
                first[field, strip, head : head + TILE] = jnp.where(sub + place > 0, edge, 0.0)
        force[strip, : head - TILE] = jnp.zeros((head - TILE, LANES), jnp.float32)
        force[strip, last + TILE :] = jnp.zeros((head - TILE, LANES), jnp.float32)
        force[strip, head - TILE : head] = (TIME_STEP * SPEED_SCALE) * force_low_ref[:, span]
        force[strip, head:last] = (TIME_STEP * SPEED_SCALE) * force_ref[:, span]
        force[strip, last : last + TILE] = (TIME_STEP * SPEED_SCALE) * force_high_ref[:, span]

    def west(values):
        turned = [pltpu.roll(value, 1, 1) for value in values]
        return [jnp.where(left, turned[i - 1], turned[i]) for i in range(strips)]

    def east(values):
        turned = [pltpu.roll(value, LANES - 1, 1) for value in values]
        return [jnp.where(right, turned[(i + 1) % strips], turned[i]) for i in range(strips)]

    def at(block):
        return pl.ds(pl.multiple_of(TILE * (block + MARGIN - 1), TILE), TILE)

    def load(source, field, block, offset=0):
        if offset == 0:
            return [source[field, strip, at(block)] for strip in range(strips)]
        return [source[field, strip, pl.ds(TILE * (block + MARGIN - 1) + offset, TILE)] for strip in range(strips)]

    def each(function, *lists):
        return [function(*items) for items in zip(*lists)]

    def keep(target, field, block, values):
        for strip in range(strips):
            target[field, strip, at(block)] = values[strip]

    def give(field, block, values):
        rows_here = pl.ds(pl.multiple_of(TILE * (block - 1), TILE), TILE)
        for strip in range(strips):
            value = values[strip] * (1.0 / HEIGHT_SCALE) - 1.0 if field % 3 == 0 else values[strip] * (1.0 / SPEED_SCALE)
            result[field, rows_here, strip * LANES : (strip + 1) * LANES] = value

    def shift_heights(source, block):
        for layer in range(2):
            keep(shifted, layer, block, west(load(source, 3 * layer, block)))

    def flux_along(source, block):
        for layer in range(2):
            base = 3 * layer
            flux = each(lambda u, t, w: u * (t + w), load(source, base + 1, block), load(source, base, block), load(shifted, layer, block))
            keep(spread, layer, block, each(lambda e, f: e - f, east(flux), flux))

    def heights(source, target, block):
        for layer in range(2):
            base = 3 * layer
            thick = load(source, base, block)
            flux_y = each(lambda v, t, b: v * (t + b), load(source, base + 2, block), thick, load(source, base, block, -1))
            above_flux = each(lambda v, t, a: v * (t + a), load(source, base + 2, block, 1), thick, load(source, base, block, 1))
            new = each(lambda h, d, a, y: (h - d) - (a - y), thick, load(spread, layer, block), above_flux, flux_y)
            keep(target, base, block, new)

    def speeds(source, target, block, store):
        row = (sub + ((block - 1) * TILE + place * rows)).astype(jnp.float32)
        coriolis_u = (0.25 * TIME_STEP) * (CORIOLIS_MEAN + (row * (1.0 / total) - 0.5))
        coriolis_v = (0.25 * TIME_STEP) * (CORIOLIS_MEAN + ((row - 0.5) * (1.0 / total) - 0.5))
        upper, lower = load(target, 0, block), load(target, 3, block)
        below_upper, below_lower = load(target, 0, block, -1), load(target, 3, block, -1)
        for layer in range(2):
            base = 3 * layer
            if layer == 0:
                pressure = each(lambda a, b: a + b, upper, lower)
                below_pressure = each(lambda a, b: a + b, below_upper, below_lower)
            else:
                pressure = each(lambda a, b: DENSITY_RATIO * a + b, upper, lower)
                below_pressure = each(lambda a, b: DENSITY_RATIO * a + b, below_upper, below_lower)
            speed_u = load(source, base + 1, block)
            speed_v = load(source, base + 2, block)
            turn_v = each(lambda v, a: coriolis_u * (v + a), speed_v, load(source, base + 2, block, 1))
            if layer == 0:
                forced = [speed_u[strip] + force[strip, at(block)] for strip in range(strips)]
            else:
                forced = [(1.0 - TIME_STEP * DRAG_RATE) * value for value in speed_u]
            pushed = west(each(lambda t, p: t + p, turn_v, pressure))
            store(base + 1, block, each(lambda f, t, p, w: (f + (t - p)) + w, forced, turn_v, pressure, pushed))
            sum_u = each(lambda u, b: u + b, speed_u, load(source, base + 1, block, -1))
            slope = each(lambda p, b: p - b, pressure, below_pressure)
            store(base + 2, block, each(lambda v, s, es, d: (v - coriolis_v * (s + es)) - d, speed_v, sum_u, east(sum_u), slope))

    def finish(source, target, block):
        give(0, block, load(target, 0, block))
        give(3, block, load(target, 3, block))
        speeds(source, target, block, give)

    def turn(stages, first_block, turn_index, valid):
        for behind, stage in enumerate(stages):
            if valid[behind]:
                for offset in range(GROUP):
                    stage(first_block + GROUP * (turn_index - behind) + offset)

    def sweep(stages, first_block, groups):
        depth = len(stages)
        for t in range(depth - 1):
            turn(stages, first_block, t, [s <= t for s in range(depth)])

        def steady(t, carry):
            turn(stages, first_block, t, [True] * depth)
            return carry

        lax.fori_loop(depth - 1, groups, steady, 0)
        for t in range(groups, groups + depth - 1):
            turn(stages, first_block, t, [t - s < groups for s in range(depth)])

    if count == 1:
        first_block, groups = 1, blocks // GROUP
    else:
        groups = blocks // GROUP + 1
        first_block = jnp.where(place == 0, 1, jnp.where(place == count - 1, 1 - GROUP, 0))
    source, target = first, second
    for _ in range(STEPS - 1):
        stages = [
            functools.partial(shift_heights, source),
            functools.partial(flux_along, source),
            functools.partial(heights, source, target),
            functools.partial(speeds, source, target, store=functools.partial(keep, target)),
        ]
        sweep(stages, first_block, groups)

        @pl.when(place == 0)
        def _():
            for field in (2, 5):
                for strip in range(strips):
                    target[field, strip, head : head + TILE] = jnp.where(bottom, 0.0, target[field, strip, head : head + TILE])

        source, target = target, source

    def finish_behind(block):
        finish(source, target, block)

    stages = [functools.partial(shift_heights, source), functools.partial(flux_along, source), functools.partial(heights, source, target)]
    for t in range(3):
        turn(stages, 1 - GROUP, t, [s <= t for s in range(3)])
    copies = []
    slab_groups = blocks // GROUP // SLABS
    for slab in range(SLABS):
        final = slab == SLABS - 1

        def steady(t, carry):
            turn([*stages, finish_behind], 1 - GROUP, t, [True] * 4)
            return carry

        begin = 4 + slab * slab_groups
        end = blocks // GROUP + 4 if final else begin + slab_groups
        full = max(begin, min(end, blocks // GROUP + 1))
        if begin == 4:
            turn(stages, 1 - GROUP, 3, [True] * 3)
        lax.fori_loop(begin, full, steady, 0)
        for t in range(full, end):
            turn([*stages, finish_behind], 1 - GROUP, t, [t - s <= blocks // GROUP for s in range(4)])
        if slab == 0:

            @pl.when(place == 0)
            def _():
                for field in (2, 5):
                    for strip in range(strips):
                        span = slice(strip * LANES, (strip + 1) * LANES)
                        result[field, :TILE, span] = jnp.where(bottom, 0.0, result[field, :TILE, span])

        first_row = TILE * GROUP * slab_groups * slab
        end_row = rows if final else TILE * GROUP * slab_groups * (slab + 1)
        copies.append(pltpu.make_async_copy(result.at[:, first_row:end_row, :], out_ref.at[:, first_row:end_row, :], sem.at[slab]))
        copies[-1].start()
    for copy in copies:
        copy.wait()


def stencil(here, parents, edges, forcing, force_edges):
    rows, columns = forcing.shape
    fields_count = parents[0].shape[0]
    shape = (fields_count, columns // LANES, rows + 2 * MARGIN * TILE, LANES)
    vmem = pl.BlockSpec(memory_space=pltpu.VMEM)
    smem = pl.BlockSpec(memory_space=pltpu.SMEM)
    return pl.pallas_call(
        functools.partial(stencil_kernel, lax.axis_size("lat"), chunks_of(rows), len(parents)),
        out_shape=jax.ShapeDtypeStruct((fields_count, rows, columns), jnp.float32),
        in_specs=[smem] + [vmem] * (len(parents) + 5),
        out_specs=pl.BlockSpec(memory_space=pltpu.HBM),
        scratch_shapes=[
            pltpu.VMEM(shape, jnp.float32),
            pltpu.VMEM(shape, jnp.float32),
            pltpu.VMEM(shape[1:], jnp.float32),
            pltpu.VMEM((2, *shape[1:]), jnp.float32),
            pltpu.VMEM((2, *shape[1:]), jnp.float32),
            pltpu.VMEM((fields_count, rows, columns), jnp.float32),
            pltpu.SemaphoreType.DMA((SLABS,)),
        ],
        compiler_params=pltpu.CompilerParams(vmem_limit_bytes=16 << 20),
        cost_estimate=pl.CostEstimate(flops=300 * rows * columns, bytes_accessed=52 * rows * columns, transcendentals=0),
    )(here, *parents, *edges, forcing, *force_edges)


def edge_rows(block):
    rows = block.shape[-2]
    dim = block.ndim - 2
    count = lax.axis_size("lat")
    if count == 2:
        sent = lax.dynamic_slice_in_dim(block, (1 - lax.axis_index("lat")) * (rows - TILE), TILE, axis=dim)
        return swap_edges(sent)
    forward = [(i, i + 1) for i in range(count - 1)]
    backward = [(target, source) for source, target in forward]
    below = lax.ppermute(lax.slice_in_dim(block, rows - TILE, rows, axis=dim), "lat", forward)
    above = lax.ppermute(lax.slice_in_dim(block, 0, TILE, axis=dim), "lat", backward)
    return below, above


def swap_edges(sent):
    got = lax.ppermute(sent, "lat", [(0, 1), (1, 0)])
    return got, got


def by_all_to_all(block, ancestors):
    fields_count, band_rows, columns = block.shape
    count = lax.axis_size("mem")
    pieces = block.reshape(count, fields_count * band_rows // count, columns)
    spread = lax.all_to_all(pieces, "mem", split_axis=0, concat_axis=0, tiled=True)
    taken = jnp.take(spread, ancestors, axis=0, mode="clip")
    moved = lax.all_to_all(taken, "mem", split_axis=0, concat_axis=0, tiled=True)
    return moved.reshape(block.shape)


PARTS = 4
MEMBERS = 2 * PARTS
CHUNKS = (1, 1)


def chunks_of(rows):
    spans = [rows * share // sum(CHUNKS) for share in CHUNKS]
    return [(sum(spans[:c]), span) for c, span in enumerate(spans)]


def part_start(here_ref, chunk, k, rows):
    passed, span = chunk
    own = lax.rem(here_ref[0], PARTS)
    return jnp.where(here_ref[1] == 0, rows - passed - span, passed) + (own ^ k) * (span // PARTS)


def shift(values, distance):
    return lax.ppermute(values, "mem", [(i, i ^ distance) for i in range(MEMBERS)])


def small_call(kernel, outs, here, tables, arrays, left, scratch=()):
    vmem = pl.BlockSpec(memory_space=pltpu.VMEM)
    smem = pl.BlockSpec(memory_space=pltpu.SMEM)
    anywhere = pl.BlockSpec(memory_space=pl.ANY)
    moved = sum(2 * out.size * 4 for out in outs)
    return pl.pallas_call(
        kernel,
        out_shape=outs,
        in_specs=[smem] * (1 + len(tables)) + [vmem] * len(arrays) + [anywhere] * len(left),
        out_specs=[vmem if out.ndim > 1 else smem for out in outs],
        scratch_shapes=list(scratch),
        compiler_params=pltpu.CompilerParams(vmem_limit_bytes=4 << 20),
        cost_estimate=pl.CostEstimate(flops=0, bytes_accessed=moved, transcendentals=0),
    )(here, *tables, *arrays, *left)


def part_shape(block, chunk):
    return jax.ShapeDtypeStruct((block.shape[0], chunk[1] // PARTS, block.shape[2]), jnp.float32)


def cut_kernel(chunk, here_ref, block_ref, *refs):
    outs, sem = refs[-PARTS:-1], refs[-1]
    copies = []
    for k, out in enumerate(outs):
        first_row = part_start(here_ref, chunk, k + 1, block_ref.shape[1])
        rows = pl.ds(pl.multiple_of(first_row, TILE), out.shape[1])
        copies.append(pltpu.make_async_copy(block_ref.at[:, rows, :], out, sem.at[k]))
    for copy in copies:
        copy.start()
    for copy in copies:
        copy.wait()


def cut(here, block, chunk, after):
    outs = [part_shape(block, chunk)] * (PARTS - 1)
    kernel = functools.partial(cut_kernel, chunk)
    return small_call(kernel, outs, here, [], [], [block, *after], [pltpu.SemaphoreType.DMA((PARTS - 1,))])


def route_kernel(chunk, sources, count, here_ref, chosen_ref, *refs):
    source_refs, block_ref = refs[:sources], refs[sources]
    outs, sem = refs[-count - 1 : -1], refs[-1]
    first_row = part_start(here_ref, chunk, 0, block_ref.shape[1])
    rows = pl.ds(pl.multiple_of(first_row, TILE), outs[0].shape[1])
    copies = [pltpu.make_async_copy(block_ref.at[:, rows, :], out, sem.at[k]) for k, out in enumerate(outs)]
    for k, copy in enumerate(copies):
        pl.when(chosen_ref[k] == 0)(copy.start)
    for k, out in enumerate(outs):
        for j, source in enumerate(source_refs):

            @pl.when(chosen_ref[k] == j + 1)
            def _():
                out[...] = source[...]

    for k, copy in enumerate(copies):
        pl.when(chosen_ref[k] == 0)(copy.wait)


def route(here, chosen, count, block, chunk, sources, after=()):
    outs = [part_shape(block, chunk)] * count
    kernel = functools.partial(route_kernel, chunk, len(sources), count)
    return small_call(kernel, outs, here, [chosen], sources, [block, *after], [pltpu.SemaphoreType.DMA((count,))])


def edge_kernel(here_ref, *refs):
    out = refs[-1]
    own = lax.rem(here_ref[0], PARTS)
    rows = refs[0].shape[1]
    for k, source in enumerate(refs[:PARTS]):
        for place, owner, first_row in ((0, PARTS - 1, rows - TILE), (1, 0, 0)):

            @pl.when((here_ref[1] == place) & ((own ^ k) == owner))
            def _():
                out[...] = source[:, first_row : first_row + TILE, :]


def tables_kernel(here_ref, ancestors_ref, *refs):
    order_ref, given_ref, most_ref, rank_ref = refs[-4:]
    member = here_ref[0]
    half, own = member // PARTS, lax.rem(member, PARTS)
    for r in range(PARTS):
        order_ref[r] = 0
    most = 0
    for side in range(2):
        rank = 0
        for place in range(PARTS):
            p = side * PARTS + place
            need = 0
            for slot in range((1 - side) * PARTS, (2 - side) * PARTS):
                need = need | jnp.where(ancestors_ref[slot] == p, 1, 0)
            rank_ref[p] = rank

            @pl.when((need > 0) & (half == side))
            def _():
                order_ref[rank] = own ^ place

            rank = rank + need
        most = jnp.maximum(most, rank)
    most_ref[0] = most
    for k in range(PARTS):
        parent = ancestors_ref[half * PARTS + (own ^ k)]
        given_ref[k] = jnp.where(parent // PARTS == half, lax.rem(parent, PARTS) ^ own, PARTS + rank_ref[parent])


def tables_of(here, ancestors, after):
    outs = [jax.ShapeDtypeStruct((size,), jnp.int32) for size in (PARTS, PARTS, 1)]
    return small_call(tables_kernel, outs, here, [ancestors], [], after, [pltpu.SMEM((MEMBERS,), jnp.int32)])


def by_crossings(here, block, ancestors):
    chunks = chunks_of(block.shape[1])

    def spread(held):
        return [shift(part, k + 1) for k, part in enumerate(held)]

    held = cut(here, block, chunks[0], ())
    shared = spread(held)
    order, given_index, most = tables_of(here, ancestors, held[:1])
    groups = lax.axis_size("groups")
    other = most
    for _ in range(groups - 1):
        other = lax.ppermute(other, "groups", [(i, (i + 1) % groups) for i in range(groups)])
        most = jnp.maximum(most, other)

    def plan(rounds, here, block, shared, order, given_index):
        crossed, final = (), []
        for c, chunk in enumerate(chunks):
            sent = route(here, order, rounds, block, chunk, shared, crossed[:1])
            following = ()
            if c + 1 < len(chunks):
                following = spread(cut(here, block, chunks[c + 1], (*shared, sent[0])))
            crossed = [shift(part, PARTS) for part in sent]
            given = route(here, given_index, PARTS, block, chunk, [*shared, *crossed])
            final.append([given[0]] + [shift(given[k], k) for k in range(1, PARTS)])
            shared = following
        edge_shape = jax.ShapeDtypeStruct((block.shape[0], TILE, block.shape[2]), jnp.float32)
        edge = small_call(edge_kernel, [edge_shape], here, [], final[0], [])[0]
        return [part for parts in final for part in parts], swap_edges(edge)[0]

    branches = [functools.partial(plan, rounds) for rounds in range(2, PARTS + 1)]
    return lax.switch(jnp.clip(most[0] - 2, 0, PARTS - 2), branches, here, block, shared, order, given_index)


def on_device(ensemble, forcing_table, ancestors, selector):
    rows = ensemble.shape[2]
    block = ensemble.reshape(ensemble.shape[1:])
    here = jnp.stack([lax.axis_index("mem"), lax.axis_index("lat")]).astype(jnp.int32)
    forcing = lax.dynamic_index_in_dim(forcing_table, selector[0], 0, keepdims=False)
    force_edges = edge_rows(forcing)
    if lax.axis_size("mem") == MEMBERS and lax.axis_size("lat") == 2 and rows % (sum(CHUNKS) * PARTS * TILE) == 0:
        parents, edge = by_crossings(here, block, ancestors)
        edges = (edge, edge)
    else:
        parents = [by_all_to_all(block, ancestors)]
        edges = edge_rows(parents[0])
    return stencil(here, parents, edges, forcing, force_edges).reshape(ensemble.shape)


def solution(mesh):
    placed = (
        P(("groups", "mem"), None, "lat", None),
        P(None, "lat", None),
        P("groups"),
        P(("groups", "mem")),
    )
    return jax.shard_map(
        on_device,
        mesh=mesh,
        in_specs=placed,
        out_specs=P(("groups", "mem"), None, "lat", None),
        check_vma=False,
    )
```

```python
import functools

import jax
import jax.numpy as jnp
from jax import lax
from jax.experimental import pallas as pl
from jax.experimental.pallas import tpu as pltpu
from jax.sharding import PartitionSpec as P

STEPS = 3


TIME_STEP = 0.25
DENSITY_RATIO = 0.9
DRAG_RATE = 0.1
CORIOLIS_MEAN = 0.5

TILE = 8
LANES = 128
SLABS = 2
GROUP = 4
MARGIN = 5


HEIGHT_SCALE = TIME_STEP * TIME_STEP / 2
SPEED_SCALE = TIME_STEP / 2


def stencil_kernel(count, chunks, pieces, here_ref, *refs):
    parent_refs = refs[:pieces]
    low_ref, high_ref, force_ref, force_low_ref, force_high_ref, out_ref = refs[pieces : pieces + 6]
    first, second, force, shifted, spread, result, sem = refs[pieces + 6 :]
    rows, columns = force_ref.shape
    blocks = rows // TILE
    strips = columns // LANES
    place = here_ref[1]
    total = float(rows * count)
    tile = (TILE, LANES)
    sub = lax.broadcasted_iota(jnp.int32, tile, 0)
    lane = lax.broadcasted_iota(jnp.int32, tile, 1)
    bottom = sub == 0
    left = lane == 0
    right = lane == LANES - 1
    head = MARGIN * TILE
    last = head + rows

    def scaled(field, value):
        return HEIGHT_SCALE + HEIGHT_SCALE * value if field % 3 == 0 else SPEED_SCALE * value

    for strip in range(strips):
        span = slice(strip * LANES, (strip + 1) * LANES)
        for field in range(6):
            low = scaled(field, jnp.where(place > 0, low_ref[field, :, span], 0.0))
            high = scaled(field, jnp.where(place < count - 1, high_ref[field, :, span], 0.0))
            for buffer in (first, second):
                buffer[field, strip, : head - TILE] = jnp.zeros((head - TILE, LANES), jnp.float32)
                buffer[field, strip, last + TILE :] = jnp.zeros((head - TILE, LANES), jnp.float32)
                buffer[field, strip, head - TILE : head] = low
                buffer[field, strip, last : last + TILE] = high
            for piece, parent_ref in enumerate(parent_refs):
                height = parent_ref.shape[1]
                first_row = head if pieces == 1 else head + part_start(here_ref, chunks[piece // PARTS], piece % PARTS, rows)
                span_rows = pl.ds(pl.multiple_of(first_row, TILE), height)
                first[field, strip, span_rows] = scaled(field, parent_ref[field, :, span])
            if field % 3 == 2:
                edge = first[field, strip, head : head + TILE]
                first[field, strip, head : head + TILE] = jnp.where(sub + place > 0, edge, 0.0)
        force[strip, : head - TILE] = jnp.zeros((head - TILE, LANES), jnp.float32)
        force[strip, last + TILE :] = jnp.zeros((head - TILE, LANES), jnp.float32)
        force[strip, head - TILE : head] = (TIME_STEP * SPEED_SCALE) * force_low_ref[:, span]
        force[strip, head:last] = (TIME_STEP * SPEED_SCALE) * force_ref[:, span]
        force[strip, last : last + TILE] = (TIME_STEP * SPEED_SCALE) * force_high_ref[:, span]

    def west(values):
        turned = [pltpu.roll(value, 1, 1) for value in values]
        return [jnp.where(left, turned[i - 1], turned[i]) for i in range(strips)]

    def east(values):
        turned = [pltpu.roll(value, LANES - 1, 1) for value in values]
        return [jnp.where(right, turned[(i + 1) % strips], turned[i]) for i in range(strips)]

    def at(block):
        return pl.ds(pl.multiple_of(TILE * (block + MARGIN - 1), TILE), TILE)

    def load(source, field, block, offset=0):
        if offset == 0:
            return [source[field, strip, at(block)] for strip in range(strips)]
        return [source[field, strip, pl.ds(TILE * (block + MARGIN - 1) + offset, TILE)] for strip in range(strips)]

    def each(function, *lists):
        return [function(*items) for items in zip(*lists)]

    def keep(target, field, block, values):
        for strip in range(strips):
            target[field, strip, at(block)] = values[strip]

    def give(field, block, values):
        rows_here = pl.ds(pl.multiple_of(TILE * (block - 1), TILE), TILE)
        for strip in range(strips):
            value = values[strip] * (1.0 / HEIGHT_SCALE) - 1.0 if field % 3 == 0 else values[strip] * (1.0 / SPEED_SCALE)
            result[field, rows_here, strip * LANES : (strip + 1) * LANES] = value

    def shift_heights(source, block):
        for layer in range(2):
            keep(shifted, layer, block, west(load(source, 3 * layer, block)))

    def flux_along(source, block):
        for layer in range(2):
            base = 3 * layer
            flux = each(lambda u, t, w: u * (t + w), load(source, base + 1, block), load(source, base, block), load(shifted, layer, block))
            keep(spread, layer, block, each(lambda e, f: e - f, east(flux), flux))

    def heights(source, target, block):
        for layer in range(2):
            base = 3 * layer
            thick = load(source, base, block)
            flux_y = each(lambda v, t, b: v * (t + b), load(source, base + 2, block), thick, load(source, base, block, -1))
            above_flux = each(lambda v, t, a: v * (t + a), load(source, base + 2, block, 1), thick, load(source, base, block, 1))
            new = each(lambda h, d, a, y: (h - d) - (a - y), thick, load(spread, layer, block), above_flux, flux_y)
            keep(target, base, block, new)

    def speeds(source, target, block, store):
        row = (sub + ((block - 1) * TILE + place * rows)).astype(jnp.float32)
        coriolis_u = (0.25 * TIME_STEP) * (CORIOLIS_MEAN + (row * (1.0 / total) - 0.5))
        coriolis_v = (0.25 * TIME_STEP) * (CORIOLIS_MEAN + ((row - 0.5) * (1.0 / total) - 0.5))
        upper, lower = load(target, 0, block), load(target, 3, block)
        below_upper, below_lower = load(target, 0, block, -1), load(target, 3, block, -1)
        for layer in range(2):
            base = 3 * layer
            if layer == 0:
                pressure = each(lambda a, b: a + b, upper, lower)
                below_pressure = each(lambda a, b: a + b, below_upper, below_lower)
            else:
                pressure = each(lambda a, b: DENSITY_RATIO * a + b, upper, lower)
                below_pressure = each(lambda a, b: DENSITY_RATIO * a + b, below_upper, below_lower)
            speed_u = load(source, base + 1, block)
            speed_v = load(source, base + 2, block)
            turn_v = each(lambda v, a: coriolis_u * (v + a), speed_v, load(source, base + 2, block, 1))
            if layer == 0:
                forced = [speed_u[strip] + force[strip, at(block)] for strip in range(strips)]
            else:
                forced = [(1.0 - TIME_STEP * DRAG_RATE) * value for value in speed_u]
            pushed = west(each(lambda t, p: t + p, turn_v, pressure))
            store(base + 1, block, each(lambda f, t, p, w: (f + (t - p)) + w, forced, turn_v, pressure, pushed))
            sum_u = each(lambda u, b: u + b, speed_u, load(source, base + 1, block, -1))
            slope = each(lambda p, b: p - b, pressure, below_pressure)
            store(base + 2, block, each(lambda v, s, es, d: (v - coriolis_v * (s + es)) - d, speed_v, sum_u, east(sum_u), slope))

    def finish(source, target, block):
        give(0, block, load(target, 0, block))
        give(3, block, load(target, 3, block))
        speeds(source, target, block, give)

    def turn(stages, first_block, turn_index, valid):
        for behind, stage in reversed(list(enumerate(stages))):
            if valid[behind]:
                for offset in range(GROUP):
                    stage(first_block + GROUP * (turn_index - behind) + offset)

    def sweep(stages, first_block, groups):
        depth = len(stages)
        for t in range(depth - 1):
            turn(stages, first_block, t, [s <= t for s in range(depth)])

        def steady(t, carry):
            turn(stages, first_block, t, [True] * depth)
            return carry

        lax.fori_loop(depth - 1, groups, steady, 0)
        for t in range(groups, groups + depth - 1):
            turn(stages, first_block, t, [t - s < groups for s in range(depth)])

    if count == 1:
        first_block, groups = 1, blocks // GROUP
    else:
        groups = blocks // GROUP + 1
        first_block = jnp.where(place == 0, 1, jnp.where(place == count - 1, 1 - GROUP, 0))
    source, target = first, second
    for _ in range(STEPS - 1):
        stages = [
            functools.partial(shift_heights, source),
            functools.partial(flux_along, source),
            functools.partial(heights, source, target),
            functools.partial(speeds, source, target, store=functools.partial(keep, target)),
        ]
        sweep(stages, first_block, groups)

        @pl.when(place == 0)
        def _():
            for field in (2, 5):
                for strip in range(strips):
                    target[field, strip, head : head + TILE] = jnp.where(bottom, 0.0, target[field, strip, head : head + TILE])

        source, target = target, source

    def finish_behind(block):
        finish(source, target, block)

    stages = [functools.partial(shift_heights, source), functools.partial(flux_along, source), functools.partial(heights, source, target)]
    for t in range(3):
        turn(stages, 1 - GROUP, t, [s <= t for s in range(3)])
    copies = []
    slab_groups = blocks // GROUP // SLABS
    for slab in range(SLABS):
        final = slab == SLABS - 1

        def steady(t, carry):
            turn([*stages, finish_behind], 1 - GROUP, t, [True] * 4)
            return carry

        begin = 4 + slab * slab_groups
        end = blocks // GROUP + 4 if final else begin + slab_groups
        full = max(begin, min(end, blocks // GROUP + 1))
        if begin == 4:
            turn(stages, 1 - GROUP, 3, [True] * 3)
        lax.fori_loop(begin, full, steady, 0)
        for t in range(full, end):
            turn([*stages, finish_behind], 1 - GROUP, t, [t - s <= blocks // GROUP for s in range(4)])
        if slab == 0:

            @pl.when(place == 0)
            def _():
                for field in (2, 5):
                    for strip in range(strips):
                        span = slice(strip * LANES, (strip + 1) * LANES)
                        result[field, :TILE, span] = jnp.where(bottom, 0.0, result[field, :TILE, span])

        first_row = TILE * GROUP * slab_groups * slab
        end_row = rows if final else TILE * GROUP * slab_groups * (slab + 1)
        copies.append(pltpu.make_async_copy(result.at[:, first_row:end_row, :], out_ref.at[:, first_row:end_row, :], sem.at[slab]))
        copies[-1].start()
    for copy in copies:
        copy.wait()


def stencil(here, parents, edges, forcing, force_edges):
    rows, columns = forcing.shape
    fields_count = parents[0].shape[0]
    shape = (fields_count, columns // LANES, rows + 2 * MARGIN * TILE, LANES)
    vmem = pl.BlockSpec(memory_space=pltpu.VMEM)
    smem = pl.BlockSpec(memory_space=pltpu.SMEM)
    return pl.pallas_call(
        functools.partial(stencil_kernel, lax.axis_size("lat"), chunks_of(rows), len(parents)),
        out_shape=jax.ShapeDtypeStruct((fields_count, rows, columns), jnp.float32),
        in_specs=[smem] + [vmem] * (len(parents) + 5),
        out_specs=pl.BlockSpec(memory_space=pltpu.HBM),
        scratch_shapes=[
            pltpu.VMEM(shape, jnp.float32),
            pltpu.VMEM(shape, jnp.float32),
            pltpu.VMEM(shape[1:], jnp.float32),
            pltpu.VMEM((2, *shape[1:]), jnp.float32),
            pltpu.VMEM((2, *shape[1:]), jnp.float32),
            pltpu.VMEM((fields_count, rows, columns), jnp.float32),
            pltpu.SemaphoreType.DMA((SLABS,)),
        ],
        compiler_params=pltpu.CompilerParams(vmem_limit_bytes=16 << 20),
        cost_estimate=pl.CostEstimate(flops=300 * rows * columns, bytes_accessed=52 * rows * columns, transcendentals=0),
    )(here, *parents, *edges, forcing, *force_edges)


def edge_rows(block):
    rows = block.shape[-2]
    dim = block.ndim - 2
    count = lax.axis_size("lat")
    if count == 2:
        sent = lax.dynamic_slice_in_dim(block, (1 - lax.axis_index("lat")) * (rows - TILE), TILE, axis=dim)
        return swap_edges(sent)
    forward = [(i, i + 1) for i in range(count - 1)]
    backward = [(target, source) for source, target in forward]
    below = lax.ppermute(lax.slice_in_dim(block, rows - TILE, rows, axis=dim), "lat", forward)
    above = lax.ppermute(lax.slice_in_dim(block, 0, TILE, axis=dim), "lat", backward)
    return below, above


def swap_edges(sent):
    got = lax.ppermute(sent, "lat", [(0, 1), (1, 0)])
    return got, got


def by_all_to_all(block, ancestors):
    fields_count, band_rows, columns = block.shape
    count = lax.axis_size("mem")
    pieces = block.reshape(count, fields_count * band_rows // count, columns)
    spread = lax.all_to_all(pieces, "mem", split_axis=0, concat_axis=0, tiled=True)
    taken = jnp.take(spread, ancestors, axis=0, mode="clip")
    moved = lax.all_to_all(taken, "mem", split_axis=0, concat_axis=0, tiled=True)
    return moved.reshape(block.shape)


PARTS = 4
MEMBERS = 2 * PARTS
CHUNKS = (1, 1)


def chunks_of(rows):
    spans = [rows * share // sum(CHUNKS) for share in CHUNKS]
    return [(sum(spans[:c]), span) for c, span in enumerate(spans)]


def part_start(here_ref, chunk, k, rows):
    passed, span = chunk
    own = lax.rem(here_ref[0], PARTS)
    return jnp.where(here_ref[1] == 0, rows - passed - span, passed) + (own ^ k) * (span // PARTS)


def shift(values, distance):
    return lax.ppermute(values, "mem", [(i, i ^ distance) for i in range(MEMBERS)])


def small_call(kernel, outs, here, tables, arrays, left, scratch=()):
    vmem = pl.BlockSpec(memory_space=pltpu.VMEM)
    smem = pl.BlockSpec(memory_space=pltpu.SMEM)
    anywhere = pl.BlockSpec(memory_space=pl.ANY)
    moved = sum(2 * out.size * 4 for out in outs)
    return pl.pallas_call(
        kernel,
        out_shape=outs,
        in_specs=[smem] * (1 + len(tables)) + [vmem] * len(arrays) + [anywhere] * len(left),
        out_specs=[vmem if out.ndim > 1 else smem for out in outs],
        scratch_shapes=list(scratch),
        compiler_params=pltpu.CompilerParams(vmem_limit_bytes=4 << 20),
        cost_estimate=pl.CostEstimate(flops=0, bytes_accessed=moved, transcendentals=0),
    )(here, *tables, *arrays, *left)


def part_shape(block, chunk):
    return jax.ShapeDtypeStruct((block.shape[0], chunk[1] // PARTS, block.shape[2]), jnp.float32)


def cut_kernel(chunk, here_ref, block_ref, *refs):
    outs, sem = refs[-PARTS:-1], refs[-1]
    copies = []
    for k, out in enumerate(outs):
        first_row = part_start(here_ref, chunk, k + 1, block_ref.shape[1])
        rows = pl.ds(pl.multiple_of(first_row, TILE), out.shape[1])
        copies.append(pltpu.make_async_copy(block_ref.at[:, rows, :], out, sem.at[k]))
    for copy in copies:
        copy.start()
    for copy in copies:
        copy.wait()


def cut(here, block, chunk, after):
    outs = [part_shape(block, chunk)] * (PARTS - 1)
    kernel = functools.partial(cut_kernel, chunk)
    return small_call(kernel, outs, here, [], [], [block, *after], [pltpu.SemaphoreType.DMA((PARTS - 1,))])


def route_kernel(chunk, sources, count, here_ref, chosen_ref, *refs):
    source_refs, block_ref = refs[:sources], refs[sources]
    outs, sem = refs[-count - 1 : -1], refs[-1]
    first_row = part_start(here_ref, chunk, 0, block_ref.shape[1])
    rows = pl.ds(pl.multiple_of(first_row, TILE), outs[0].shape[1])
    copies = [pltpu.make_async_copy(block_ref.at[:, rows, :], out, sem.at[k]) for k, out in enumerate(outs)]
    for k, copy in enumerate(copies):
        pl.when(chosen_ref[k] == 0)(copy.start)
    for k, out in enumerate(outs):
        for j, source in enumerate(source_refs):

            @pl.when(chosen_ref[k] == j + 1)
            def _():
                out[...] = source[...]

    for k, copy in enumerate(copies):
        pl.when(chosen_ref[k] == 0)(copy.wait)


def route(here, chosen, count, block, chunk, sources, after=()):
    outs = [part_shape(block, chunk)] * count
    kernel = functools.partial(route_kernel, chunk, len(sources), count)
    return small_call(kernel, outs, here, [chosen], sources, [block, *after], [pltpu.SemaphoreType.DMA((count,))])


def edge_kernel(here_ref, *refs):
    out = refs[-1]
    own = lax.rem(here_ref[0], PARTS)
    rows = refs[0].shape[1]
    for k, source in enumerate(refs[:PARTS]):
        for place, owner, first_row in ((0, PARTS - 1, rows - TILE), (1, 0, 0)):

            @pl.when((here_ref[1] == place) & ((own ^ k) == owner))
            def _():
                out[...] = source[:, first_row : first_row + TILE, :]


def tables_kernel(here_ref, ancestors_ref, *refs):
    order_ref, given_ref, most_ref, rank_ref = refs[-4:]
    member = here_ref[0]
    half, own = member // PARTS, lax.rem(member, PARTS)
    for r in range(PARTS):
        order_ref[r] = 0
    most = 0
    for side in range(2):
        rank = 0
        for place in range(PARTS):
            p = side * PARTS + place
            need = 0
            for slot in range((1 - side) * PARTS, (2 - side) * PARTS):
                need = need | jnp.where(ancestors_ref[slot] == p, 1, 0)
            rank_ref[p] = rank

            @pl.when((need > 0) & (half == side))
            def _():
                order_ref[rank] = own ^ place

            rank = rank + need
        most = jnp.maximum(most, rank)
    most_ref[0] = most
    for k in range(PARTS):
        parent = ancestors_ref[half * PARTS + (own ^ k)]
        given_ref[k] = jnp.where(parent // PARTS == half, lax.rem(parent, PARTS) ^ own, PARTS + rank_ref[parent])


def tables_of(here, ancestors, after):
    outs = [jax.ShapeDtypeStruct((size,), jnp.int32) for size in (PARTS, PARTS, 1)]
    return small_call(tables_kernel, outs, here, [ancestors], [], after, [pltpu.SMEM((MEMBERS,), jnp.int32)])


def by_crossings(here, block, ancestors, force_edge):
    chunks = chunks_of(block.shape[1])

    def spread(held):
        return [shift(part, k + 1) for k, part in enumerate(held)]

    held = cut(here, block, chunks[0], ())
    shared = spread(held)
    order, given_index, most = tables_of(here, ancestors, held[:1])
    groups = lax.axis_size("groups")
    other = most
    for _ in range(groups - 1):
        other = lax.ppermute(other, "groups", [(i, (i + 1) % groups) for i in range(groups)])
        most = jnp.maximum(most, other)

    def plan(rounds, here, block, shared, order, given_index, force_edge):
        crossed, final = (), []
        for c, chunk in enumerate(chunks):
            sent = route(here, order, rounds, block, chunk, shared, crossed if rounds == 2 else crossed[:1])
            following = ()
            if c + 1 < len(chunks):
                following = spread(cut(here, block, chunks[c + 1], (*shared, sent[0])))
            crossed = [shift(part, PARTS) for part in sent]
            given = route(here, given_index, PARTS, block, chunk, [*shared, *crossed])
            final.append([given[0]] + [shift(given[k], k) for k in range(1, PARTS)])
            shared = following
        edge_shape = jax.ShapeDtypeStruct((block.shape[0], TILE, block.shape[2]), jnp.float32)
        edge = small_call(edge_kernel, [edge_shape], here, [], final[0], [])[0]
        return [part for parts in final for part in parts], swap_edges(edge)[0], force_edge

    branches = [functools.partial(plan, rounds) for rounds in range(2, PARTS + 1)]
    return lax.switch(jnp.clip(most[0] - 2, 0, PARTS - 2), branches, here, block, shared, order, given_index, force_edge)


def on_device(ensemble, forcing_table, ancestors, selector):
    rows = ensemble.shape[2]
    block = ensemble.reshape(ensemble.shape[1:])
    here = jnp.stack([lax.axis_index("mem"), lax.axis_index("lat")]).astype(jnp.int32)
    forcing = lax.dynamic_index_in_dim(forcing_table, selector[0], 0, keepdims=False)
    force_edges = edge_rows(forcing)
    if lax.axis_size("mem") == MEMBERS and lax.axis_size("lat") == 2 and rows % (sum(CHUNKS) * PARTS * TILE) == 0:
        parents, edge, force_edge = by_crossings(here, block, ancestors, force_edges[0])
        edges, force_edges = (edge, edge), (force_edge, force_edge)
    else:
        parents = [by_all_to_all(block, ancestors)]
        edges = edge_rows(parents[0])
    return stencil(here, parents, edges, forcing, force_edges).reshape(ensemble.shape)


def solution(mesh):
    placed = (
        P(("groups", "mem"), None, "lat", None),
        P(None, "lat", None),
        P("groups"),
        P(("groups", "mem")),
    )
    return jax.shard_map(
        on_device,
        mesh=mesh,
        in_specs=placed,
        out_specs=P(("groups", "mem"), None, "lat", None),
        check_vma=False,
    )
```

```python
import functools

import jax
import jax.numpy as jnp
from jax import lax
from jax.experimental import pallas as pl
from jax.experimental.pallas import tpu as pltpu
from jax.sharding import PartitionSpec as P

STEPS = 3


TIME_STEP = 0.25
DENSITY_RATIO = 0.9
DRAG_RATE = 0.1
CORIOLIS_MEAN = 0.5

TILE = 8
LANES = 128
SLABS = 2
GROUP = 4
MARGIN = 5


HEIGHT_SCALE = TIME_STEP * TIME_STEP / 2
SPEED_SCALE = TIME_STEP / 2


def stencil_kernel(count, chunks, pieces, here_ref, *refs):
    parent_refs = refs[:pieces]
    low_ref, high_ref, force_ref, force_low_ref, force_high_ref, out_ref = refs[pieces : pieces + 6]
    first, second, force, shifted, spread, result, sem = refs[pieces + 6 :]
    rows, columns = force_ref.shape
    blocks = rows // TILE
    strips = columns // LANES
    place = here_ref[1]
    total = float(rows * count)
    tile = (TILE, LANES)
    sub = lax.broadcasted_iota(jnp.int32, tile, 0)
    lane = lax.broadcasted_iota(jnp.int32, tile, 1)
    bottom = sub == 0
    left = lane == 0
    right = lane == LANES - 1
    head = MARGIN * TILE
    last = head + rows

    def scaled(field, value):
        return HEIGHT_SCALE + HEIGHT_SCALE * value if field % 3 == 0 else SPEED_SCALE * value

    for strip in range(strips):
        span = slice(strip * LANES, (strip + 1) * LANES)
        for field in range(6):
            low = scaled(field, jnp.where(place > 0, low_ref[field, :, span], 0.0))
            high = scaled(field, jnp.where(place < count - 1, high_ref[field, :, span], 0.0))
            for buffer in (first, second):
                buffer[field, strip, : head - TILE] = jnp.zeros((head - TILE, LANES), jnp.float32)
                buffer[field, strip, last + TILE :] = jnp.zeros((head - TILE, LANES), jnp.float32)
                buffer[field, strip, head - TILE : head] = low
                buffer[field, strip, last : last + TILE] = high
            for piece, parent_ref in enumerate(parent_refs):
                height = parent_ref.shape[1]
                first_row = head if pieces == 1 else head + part_start(here_ref, chunks[piece // PARTS], piece % PARTS, rows)
                span_rows = pl.ds(pl.multiple_of(first_row, TILE), height)
                first[field, strip, span_rows] = scaled(field, parent_ref[field, :, span])
            if field % 3 == 2:
                edge = first[field, strip, head : head + TILE]
                first[field, strip, head : head + TILE] = jnp.where(sub + place > 0, edge, 0.0)
        force[strip, : head - TILE] = jnp.zeros((head - TILE, LANES), jnp.float32)
        force[strip, last + TILE :] = jnp.zeros((head - TILE, LANES), jnp.float32)
        force[strip, head - TILE : head] = (TIME_STEP * SPEED_SCALE) * force_low_ref[:, span]
        force[strip, head:last] = (TIME_STEP * SPEED_SCALE) * force_ref[:, span]
        force[strip, last : last + TILE] = (TIME_STEP * SPEED_SCALE) * force_high_ref[:, span]

    def west(values):
        turned = [pltpu.roll(value, 1, 1) for value in values]
        return [jnp.where(left, turned[i - 1], turned[i]) for i in range(strips)]

    def east(values):
        turned = [pltpu.roll(value, LANES - 1, 1) for value in values]
        return [jnp.where(right, turned[(i + 1) % strips], turned[i]) for i in range(strips)]

    def at(block):
        return pl.ds(pl.multiple_of(TILE * (block + MARGIN - 1), TILE), TILE)

    def load(source, field, block, offset=0):
        if offset == 0:
            return [source[field, strip, at(block)] for strip in range(strips)]
        return [source[field, strip, pl.ds(TILE * (block + MARGIN - 1) + offset, TILE)] for strip in range(strips)]

    def each(function, *lists):
        return [function(*items) for items in zip(*lists)]

    def keep(target, field, block, values):
        for strip in range(strips):
            target[field, strip, at(block)] = values[strip]

    def give(field, block, values):
        rows_here = pl.ds(pl.multiple_of(TILE * (block - 1), TILE), TILE)
        for strip in range(strips):
            value = values[strip] * (1.0 / HEIGHT_SCALE) - 1.0 if field % 3 == 0 else values[strip] * (1.0 / SPEED_SCALE)
            result[field, rows_here, strip * LANES : (strip + 1) * LANES] = value

    def shift_heights(source, block):
        for layer in range(2):
            keep(shifted, layer, block, west(load(source, 3 * layer, block)))

    def flux_along(source, block):
        for layer in range(2):
            base = 3 * layer
            flux = each(lambda u, t, w: u * (t + w), load(source, base + 1, block), load(source, base, block), load(shifted, layer, block))
            keep(spread, layer, block, each(lambda e, f: e - f, east(flux), flux))

    def heights(source, target, block):
        for layer in range(2):
            base = 3 * layer
            thick = load(source, base, block)
            flux_y = each(lambda v, t, b: v * (t + b), load(source, base + 2, block), thick, load(source, base, block, -1))
            above_flux = each(lambda v, t, a: v * (t + a), load(source, base + 2, block, 1), thick, load(source, base, block, 1))
            new = each(lambda h, d, a, y: (h - d) - (a - y), thick, load(spread, layer, block), above_flux, flux_y)
            keep(target, base, block, new)

    def speeds(source, target, block, store):
        row = (sub + ((block - 1) * TILE + place * rows)).astype(jnp.float32)
        coriolis_u = (0.25 * TIME_STEP) * (CORIOLIS_MEAN + (row * (1.0 / total) - 0.5))
        coriolis_v = (0.25 * TIME_STEP) * (CORIOLIS_MEAN + ((row - 0.5) * (1.0 / total) - 0.5))
        upper, lower = load(target, 0, block), load(target, 3, block)
        below_upper, below_lower = load(target, 0, block, -1), load(target, 3, block, -1)
        for layer in range(2):
            base = 3 * layer
            if layer == 0:
                pressure = each(lambda a, b: a + b, upper, lower)
                below_pressure = each(lambda a, b: a + b, below_upper, below_lower)
            else:
                pressure = each(lambda a, b: DENSITY_RATIO * a + b, upper, lower)
                below_pressure = each(lambda a, b: DENSITY_RATIO * a + b, below_upper, below_lower)
            speed_u = load(source, base + 1, block)
            speed_v = load(source, base + 2, block)
            turn_v = each(lambda v, a: coriolis_u * (v + a), speed_v, load(source, base + 2, block, 1))
            if layer == 0:
                forced = [speed_u[strip] + force[strip, at(block)] for strip in range(strips)]
            else:
                forced = [(1.0 - TIME_STEP * DRAG_RATE) * value for value in speed_u]
            pushed = west(each(lambda t, p: t + p, turn_v, pressure))
            store(base + 1, block, each(lambda f, t, p, w: (f + (t - p)) + w, forced, turn_v, pressure, pushed))
            sum_u = each(lambda u, b: u + b, speed_u, load(source, base + 1, block, -1))
            slope = each(lambda p, b: p - b, pressure, below_pressure)
            store(base + 2, block, each(lambda v, s, es, d: (v - coriolis_v * (s + es)) - d, speed_v, sum_u, east(sum_u), slope))

    def finish(source, target, block):
        give(0, block, load(target, 0, block))
        give(3, block, load(target, 3, block))
        speeds(source, target, block, give)

    def turn(stages, first_block, turn_index, valid):
        for behind, stage in reversed(list(enumerate(stages))):
            if valid[behind]:
                for offset in range(GROUP):
                    stage(first_block + GROUP * (turn_index - behind) + offset)

    def sweep(stages, first_block, groups):
        depth = len(stages)
        for t in range(depth - 1):
            turn(stages, first_block, t, [s <= t for s in range(depth)])

        def steady(t, carry):
            turn(stages, first_block, t, [True] * depth)
            return carry

        lax.fori_loop(depth - 1, groups, steady, 0)
        for t in range(groups, groups + depth - 1):
            turn(stages, first_block, t, [t - s < groups for s in range(depth)])

    if count == 1:
        first_block, groups = 1, blocks // GROUP
    else:
        groups = blocks // GROUP + 1
        first_block = jnp.where(place == 0, 1, jnp.where(place == count - 1, 1 - GROUP, 0))
    source, target = first, second
    for _ in range(STEPS - 1):
        stages = [
            functools.partial(shift_heights, source),
            functools.partial(flux_along, source),
            functools.partial(heights, source, target),
            functools.partial(speeds, source, target, store=functools.partial(keep, target)),
        ]
        sweep(stages, first_block, groups)

        @pl.when(place == 0)
        def _():
            for field in (2, 5):
                for strip in range(strips):
                    target[field, strip, head : head + TILE] = jnp.where(bottom, 0.0, target[field, strip, head : head + TILE])

        source, target = target, source

    def finish_behind(block):
        finish(source, target, block)

    stages = [functools.partial(shift_heights, source), functools.partial(flux_along, source), functools.partial(heights, source, target)]
    for t in range(3):
        turn(stages, 1 - GROUP, t, [s <= t for s in range(3)])
    copies = []
    slab_groups = blocks // GROUP // SLABS
    for slab in range(SLABS):
        final = slab == SLABS - 1

        def steady(t, carry):
            turn([*stages, finish_behind], 1 - GROUP, t, [True] * 4)
            return carry

        begin = 4 + slab * slab_groups
        end = blocks // GROUP + 4 if final else begin + slab_groups
        full = max(begin, min(end, blocks // GROUP + 1))
        if begin == 4:
            turn(stages, 1 - GROUP, 3, [True] * 3)
        lax.fori_loop(begin, full, steady, 0)
        for t in range(full, end):
            turn([*stages, finish_behind], 1 - GROUP, t, [t - s <= blocks // GROUP for s in range(4)])
        if slab == 0:

            @pl.when(place == 0)
            def _():
                for field in (2, 5):
                    for strip in range(strips):
                        span = slice(strip * LANES, (strip + 1) * LANES)
                        result[field, :TILE, span] = jnp.where(bottom, 0.0, result[field, :TILE, span])

        first_row = TILE * GROUP * slab_groups * slab
        end_row = rows if final else TILE * GROUP * slab_groups * (slab + 1)
        copies.append(pltpu.make_async_copy(result.at[:, first_row:end_row, :], out_ref.at[:, first_row:end_row, :], sem.at[slab]))
        copies[-1].start()
    for copy in copies:
        copy.wait()


def stencil(here, parents, edges, forcing, force_edges):
    rows, columns = forcing.shape
    fields_count = parents[0].shape[0]
    shape = (fields_count, columns // LANES, rows + 2 * MARGIN * TILE, LANES)
    vmem = pl.BlockSpec(memory_space=pltpu.VMEM)
    smem = pl.BlockSpec(memory_space=pltpu.SMEM)
    return pl.pallas_call(
        functools.partial(stencil_kernel, lax.axis_size("lat"), chunks_of(rows), len(parents)),
        out_shape=jax.ShapeDtypeStruct((fields_count, rows, columns), jnp.float32),
        in_specs=[smem] + [vmem] * (len(parents) + 5),
        out_specs=pl.BlockSpec(memory_space=pltpu.HBM),
        scratch_shapes=[
            pltpu.VMEM(shape, jnp.float32),
            pltpu.VMEM(shape, jnp.float32),
            pltpu.VMEM(shape[1:], jnp.float32),
            pltpu.VMEM((2, *shape[1:]), jnp.float32),
            pltpu.VMEM((2, *shape[1:]), jnp.float32),
            pltpu.VMEM((fields_count, rows, columns), jnp.float32),
            pltpu.SemaphoreType.DMA((SLABS,)),
        ],
        compiler_params=pltpu.CompilerParams(vmem_limit_bytes=16 << 20),
        cost_estimate=pl.CostEstimate(flops=300 * rows * columns, bytes_accessed=52 * rows * columns, transcendentals=0),
    )(here, *parents, *edges, forcing, *force_edges)


def edge_rows(block):
    rows = block.shape[-2]
    dim = block.ndim - 2
    count = lax.axis_size("lat")
    if count == 2:
        sent = lax.dynamic_slice_in_dim(block, (1 - lax.axis_index("lat")) * (rows - TILE), TILE, axis=dim)
        return swap_edges(sent)
    forward = [(i, i + 1) for i in range(count - 1)]
    backward = [(target, source) for source, target in forward]
    below = lax.ppermute(lax.slice_in_dim(block, rows - TILE, rows, axis=dim), "lat", forward)
    above = lax.ppermute(lax.slice_in_dim(block, 0, TILE, axis=dim), "lat", backward)
    return below, above


def swap_edges(sent):
    got = lax.ppermute(sent, "lat", [(0, 1), (1, 0)])
    return got, got


def by_all_to_all(block, ancestors):
    fields_count, band_rows, columns = block.shape
    count = lax.axis_size("mem")
    pieces = block.reshape(count, fields_count * band_rows // count, columns)
    spread = lax.all_to_all(pieces, "mem", split_axis=0, concat_axis=0, tiled=True)
    taken = jnp.take(spread, ancestors, axis=0, mode="clip")
    moved = lax.all_to_all(taken, "mem", split_axis=0, concat_axis=0, tiled=True)
    return moved.reshape(block.shape)


PARTS = 4
MEMBERS = 2 * PARTS
CHUNKS = (1, 1)


def chunks_of(rows):
    spans = [rows * share // sum(CHUNKS) for share in CHUNKS]
    return [(sum(spans[:c]), span) for c, span in enumerate(spans)]


def part_start(here_ref, chunk, k, rows):
    passed, span = chunk
    own = lax.rem(here_ref[0], PARTS)
    return jnp.where(here_ref[1] == 0, rows - passed - span, passed) + (own ^ k) * (span // PARTS)


def shift(values, distance):
    return lax.ppermute(values, "mem", [(i, i ^ distance) for i in range(MEMBERS)])


def small_call(kernel, outs, here, tables, arrays, left, scratch=()):
    vmem = pl.BlockSpec(memory_space=pltpu.VMEM)
    smem = pl.BlockSpec(memory_space=pltpu.SMEM)
    anywhere = pl.BlockSpec(memory_space=pl.ANY)
    moved = sum(2 * out.size * 4 for out in outs)
    return pl.pallas_call(
        kernel,
        out_shape=outs,
        in_specs=[smem] * (1 + len(tables)) + [vmem] * len(arrays) + [anywhere] * len(left),
        out_specs=[vmem if out.ndim > 1 else smem for out in outs],
        scratch_shapes=list(scratch),
        compiler_params=pltpu.CompilerParams(vmem_limit_bytes=4 << 20),
        cost_estimate=pl.CostEstimate(flops=0, bytes_accessed=moved, transcendentals=0),
    )(here, *tables, *arrays, *left)


def part_shape(block, chunk):
    return jax.ShapeDtypeStruct((block.shape[0], chunk[1] // PARTS, block.shape[2]), jnp.float32)


def cut_kernel(chunk, here_ref, block_ref, *refs):
    outs, sem = refs[-PARTS:-1], refs[-1]
    copies = []
    for k, out in enumerate(outs):
        first_row = part_start(here_ref, chunk, k + 1, block_ref.shape[1])
        rows = pl.ds(pl.multiple_of(first_row, TILE), out.shape[1])
        copies.append(pltpu.make_async_copy(block_ref.at[:, rows, :], out, sem.at[k]))
    for copy in copies:
        copy.start()
    for copy in copies:
        copy.wait()


def cut(here, block, chunk, after):
    outs = [part_shape(block, chunk)] * (PARTS - 1)
    kernel = functools.partial(cut_kernel, chunk)
    return small_call(kernel, outs, here, [], [], [block, *after], [pltpu.SemaphoreType.DMA((PARTS - 1,))])


def route_kernel(chunk, sources, count, here_ref, chosen_ref, *refs):
    source_refs, block_ref = refs[:sources], refs[sources]
    outs, sem = refs[-count - 1 : -1], refs[-1]
    first_row = part_start(here_ref, chunk, 0, block_ref.shape[1])
    rows = pl.ds(pl.multiple_of(first_row, TILE), outs[0].shape[1])
    copies = [pltpu.make_async_copy(block_ref.at[:, rows, :], out, sem.at[k]) for k, out in enumerate(outs)]
    for k, copy in enumerate(copies):
        pl.when(chosen_ref[k] == 0)(copy.start)
    for k, out in enumerate(outs):
        for j, source in enumerate(source_refs):

            @pl.when(chosen_ref[k] == j + 1)
            def _():
                out[...] = source[...]

    for k, copy in enumerate(copies):
        pl.when(chosen_ref[k] == 0)(copy.wait)


def route(here, chosen, count, block, chunk, sources, after=()):
    outs = [part_shape(block, chunk)] * count
    kernel = functools.partial(route_kernel, chunk, len(sources), count)
    return small_call(kernel, outs, here, [chosen], sources, [block, *after], [pltpu.SemaphoreType.DMA((count,))])


def edge_kernel(here_ref, *refs):
    out = refs[-1]
    own = lax.rem(here_ref[0], PARTS)
    rows = refs[0].shape[1]
    for k, source in enumerate(refs[:PARTS]):
        for place, owner, first_row in ((0, PARTS - 1, rows - TILE), (1, 0, 0)):

            @pl.when((here_ref[1] == place) & ((own ^ k) == owner))
            def _():
                out[...] = source[:, first_row : first_row + TILE, :]


def tables_kernel(here_ref, ancestors_ref, *refs):
    order_ref, given_ref, most_ref, rank_ref = refs[-4:]
    member = here_ref[0]
    half, own = member // PARTS, lax.rem(member, PARTS)
    for r in range(PARTS):
        order_ref[r] = 0
    most = 0
    for side in range(2):
        rank = 0
        for place in range(PARTS):
            p = side * PARTS + place
            need = 0
            for slot in range((1 - side) * PARTS, (2 - side) * PARTS):
                need = need | jnp.where(ancestors_ref[slot] == p, 1, 0)
            rank_ref[p] = rank

            @pl.when((need > 0) & (half == side))
            def _():
                order_ref[rank] = own ^ place

            rank = rank + need
        most = jnp.maximum(most, rank)
    most_ref[0] = most
    for k in range(PARTS):
        parent = ancestors_ref[half * PARTS + (own ^ k)]
        given_ref[k] = jnp.where(parent // PARTS == half, lax.rem(parent, PARTS) ^ own, PARTS + rank_ref[parent])


def tables_of(here, ancestors, after):
    outs = [jax.ShapeDtypeStruct((size,), jnp.int32) for size in (PARTS, PARTS, 1)]
    return small_call(tables_kernel, outs, here, [ancestors], [], after, [pltpu.SMEM((MEMBERS,), jnp.int32)])


def by_crossings(here, block, ancestors, force_edge):
    chunks = chunks_of(block.shape[1])

    def spread(held):
        return [shift(part, k + 1) for k, part in enumerate(held)]

    held = cut(here, block, chunks[0], ())
    shared = spread(held)
    order, given_index, most = tables_of(here, ancestors, held[:1])
    groups = lax.axis_size("groups")
    other = most
    for _ in range(groups - 1):
        other = lax.ppermute(other, "groups", [(i, (i + 1) % groups) for i in range(groups)])
        most = jnp.maximum(most, other)

    def plan(rounds, here, block, shared, order, given_index, force_edge):
        crossed, final = (), []
        for c, chunk in enumerate(chunks):
            gate = crossed if rounds == 2 else crossed[:1]
            sent = route(here, order, rounds, block, chunk, shared, (*gate, force_edge) if c > 0 else ())
            following = ()
            if c + 1 < len(chunks):
                following = spread(cut(here, block, chunks[c + 1], (*shared, sent[0])))
            crossed = [shift(part, PARTS) for part in sent]
            given = route(here, given_index, PARTS, block, chunk, [*shared, *crossed])
            final.append([given[0]] + [shift(given[k], k) for k in range(1, PARTS)])
            shared = following
        edge_shape = jax.ShapeDtypeStruct((block.shape[0], TILE, block.shape[2]), jnp.float32)
        edge = small_call(edge_kernel, [edge_shape], here, [], final[0], [])[0]
        return [part for parts in final for part in parts], swap_edges(edge)[0]

    branches = [functools.partial(plan, rounds) for rounds in range(2, PARTS + 1)]
    return lax.switch(jnp.clip(most[0] - 2, 0, PARTS - 2), branches, here, block, shared, order, given_index, force_edge)


def on_device(ensemble, forcing_table, ancestors, selector):
    rows = ensemble.shape[2]
    block = ensemble.reshape(ensemble.shape[1:])
    here = jnp.stack([lax.axis_index("mem"), lax.axis_index("lat")]).astype(jnp.int32)
    forcing = lax.dynamic_index_in_dim(forcing_table, selector[0], 0, keepdims=False)
    force_edges = edge_rows(forcing)
    if lax.axis_size("mem") == MEMBERS and lax.axis_size("lat") == 2 and rows % (sum(CHUNKS) * PARTS * TILE) == 0:
        parents, edge = by_crossings(here, block, ancestors, force_edges[0])
        edges = (edge, edge)
    else:
        parents = [by_all_to_all(block, ancestors)]
        edges = edge_rows(parents[0])
    return stencil(here, parents, edges, forcing, force_edges).reshape(ensemble.shape)


def solution(mesh):
    placed = (
        P(("groups", "mem"), None, "lat", None),
        P(None, "lat", None),
        P("groups"),
        P(("groups", "mem")),
    )
    return jax.shard_map(
        on_device,
        mesh=mesh,
        in_specs=placed,
        out_specs=P(("groups", "mem"), None, "lat", None),
        check_vma=False,
    )
```
